128 devices in a mesh: range: 16 (over z, y), doppler: 8 (over x, core).
Axes of the slice: x: 4, y: 4, z: 4, core: 2. Of those that a mesh axis runs over, the one named last changes fastest.
Arguments:
- snapshots: bfloat16 [128, 16384, 384], P(None, ('range', 'doppler')), may hold values from -24 to 24
- steering: bfloat16 [128, 384, 256], P(('range', 'doppler')), may hold values from -0.3125 to 0.3125
- train_list: int32 [128, 128], P(('range', 'doppler')), may hold values from 0 to 127, each once within a row
- train_count: int32 [128], P(('range', 'doppler')), may hold values from 42 to 128, as said below
Outputs:
- beam_output: bfloat16 [128, 16384, 256], P(None, ('range', 'doppler'))
The draws below stay inside these ranges and needn't reach their ends.
Inputs may be any that keep to these rules, and one draw needn't show every extreme that they name: `train_count`: some bin trains on all 128 blocks and some bin on 42.
All inputs are finite; a program needn't handle non-finite values.
Results may differ from the reference program's by a relative error of at most 0.0052.
Values may be sent and summed in bfloat16 or wider, within the bound.
A program may use at most 128 MiB of HBM per device.

```python
import math
import jax
import jax.numpy as jnp
from jax import lax

DOF = 384
BEAMS = 256
BLOCK = 128
BINS = 128
NBLK = 128
GATES = 16384


def draw_snapshots(key, part):
    subkeys = jax.random.split(key, 5)
    block_total = GATES // BLOCK
    noise = jax.random.normal(subkeys[0], (BINS, GATES, DOF), jnp.float32)
    power = jnp.exp(jax.random.uniform(subkeys[1], (BINS, block_total), jnp.float32, math.log(0.4), math.log(4.0)))
    gains = jax.random.uniform(subkeys[2], (DOF,), jnp.float32, 0.5, 1.5)
    clutter = jax.random.normal(subkeys[3], (BINS, GATES), jnp.float32)
    pattern = jax.random.normal(subkeys[4], (BINS, DOF), jnp.float32) * 0.3
    level = jnp.repeat(power, BLOCK, axis=1, total_repeat_length=GATES)
    values = level[:, :, None] * (noise * gains[None, None, :] + clutter[:, :, None] * pattern[:, None, :])
    return jnp.clip(values, -24.0, 24.0).astype(jnp.bfloat16)


def draw_train_count(key, part):
    subkeys = jax.random.split(key, 2)
    block_total = GATES // BLOCK
    counts = jax.random.randint(subkeys[0], (BINS,), block_total // 3, block_total + 1)
    fullest = jax.random.randint(subkeys[1], (), 0, BINS)
    fewest = (fullest + BINS // 2) % BINS
    bin_ids = jnp.arange(BINS, dtype=jnp.int32)
    counts = jnp.where(bin_ids == fullest, block_total, counts)
    counts = jnp.where(bin_ids == fewest, block_total // 3, counts)
    return counts.astype(jnp.int32)


def block_scale(rng, extent, cuts, smallest, high):
    def one(dim, blocks):
        draws = jax.random.uniform(jax.random.fold_in(jax.random.fold_in(rng, 6), dim), (blocks,), jnp.float32, smallest / len(cuts), high / len(cuts))
        return jnp.repeat(jnp.exp(draws), extent[dim] // blocks).reshape((-1,) + (1,) * (len(extent) - dim - 1))

    level = one(*cuts[0])
    for cut in cuts[1:]:
        level = level * one(*cut)
    return level


def centred(rng, extent, scale, bound, shards=(), kind=jnp.bfloat16):
    loudness = block_scale(rng, extent, shards, -0.22, 0.18) if shards else 1.0
    values = jax.random.normal(rng, extent, jnp.float32) * scale * loudness
    return jnp.minimum(jnp.maximum(values, -bound), bound).astype(kind)


def setup_inputs(seed: int = 0) -> dict:
    arg_keys = jax.random.split(jax.random.key(seed), 5)
    snapshots = draw_snapshots(jax.random.fold_in(arg_keys[4], 71), 0)
    steering = centred(arg_keys[1], (BINS, DOF, BEAMS), DOF ** -0.5, 0.3125, ((0, 128),))
    train_list = jax.vmap(lambda own: jax.random.permutation(own, NBLK))(jax.random.split(arg_keys[2], BINS)).reshape((BINS, NBLK)).astype(jnp.int32)
    train_count = draw_train_count(jax.random.fold_in(arg_keys[4], 71), 0)
    return {"snapshots": snapshots, "steering": steering, "train_list": train_list, "train_count": train_count}


LOADING = 0.1

def cholesky_solve(factor, rhs_block):
    inner = lax.linalg.triangular_solve(factor, rhs_block, left_side=True, lower=True)
    return lax.linalg.triangular_solve(factor, inner, left_side=True, lower=True, transpose_a=True)

def one_bin(operands):
    snaps, steer, order_list, train_rows = operands
    block_total = order_list.shape[0]
    position = jnp.arange(block_total, dtype=jnp.int32)
    block_ids = jnp.arange(block_total, dtype=jnp.int32)
    matches = (order_list[:, None] == block_ids[None, :]) & (position[:, None] < train_rows)
    chosen = jnp.sum(matches.astype(jnp.int32), axis=0)
    blocks = snaps.reshape(block_total, BLOCK, DOF).astype(jnp.float32)
    masked = blocks * chosen.astype(jnp.float32)[:, None, None]
    gram_sum = jnp.einsum('nrd,nre->de', masked, blocks, precision=lax.Precision.HIGHEST)
    scale = (BLOCK * train_rows).astype(jnp.float32)
    covariance = gram_sum / scale + LOADING * jnp.eye(DOF, dtype=jnp.float32)
    factor = jnp.linalg.cholesky(covariance)
    steer_full = steer.astype(jnp.float32)
    solved = cholesky_solve(factor, steer_full)
    response = jnp.sum(steer_full * solved, axis=0)
    weights = (solved / response[None, :]).astype(jnp.bfloat16)
    return jnp.dot(snaps.astype(jnp.float32), weights.astype(jnp.float32), preferred_element_type=jnp.float32).astype(jnp.bfloat16)

def reference(snapshots, steering, train_list, train_count):
    return lax.map(one_bin, (snapshots, steering, train_list, train_count))
```

```python
import jax
import jax.numpy as jnp
from jax import lax
from jax.experimental import pallas as pl
from jax.experimental.pallas import tpu as pltpu
from jax.sharding import PartitionSpec as P

BLOCK = 128


LOADING = 0.1


def selection(train_list, train_count):
    block_total = train_list.shape[1]
    position = lax.broadcasted_iota(jnp.int32, (1, block_total, 1), 1)
    block_ids = lax.broadcasted_iota(jnp.int32, (1, 1, block_total), 2)
    matches = (train_list[:, :, None] == block_ids) & (position < train_count[:, None, None])
    return jnp.sum(matches.astype(jnp.int32), axis=1)


HI = lax.Precision.HIGHEST
T = 128
def mm(a, b, ca, cb):
    return lax.dot_general(a, b, (((ca,), (cb,)), ((), ())), precision=HI, preferred_element_type=jnp.float32)

def factor_inverse(block):
    lane = lax.broadcasted_iota(jnp.int32, (8, T), 1)
    sub = lax.broadcasted_iota(jnp.int32, (8, T), 0)
    rows = [block[8 * g:8 * g + 8, :] for g in range(T // 8)]
    for k in range(T):
        own, off = k // 8, k % 8
        row = rows[own][off:off + 1, :]
        inv = 1.0 / row[:, k:k + 1]
        scaled = jnp.where(lane[:1] == k, 1.0, row) * inv
        for g in range(own, T // 8):
            col = rows[g][:, k:k + 1]
            if g == own:
                if off == 7:
                    continue
                col = jnp.where(sub[:, :1] > off, col, 0.0)
                base = jnp.where((lane == k) & (sub > off), 0.0, rows[g])
            else:
                base = jnp.where(lane == k, 0.0, rows[g])
            rows[g] = base - col * scaled
    full = jnp.concatenate(rows, axis=0)
    i = lax.broadcasted_iota(jnp.int32, (T, T), 0)
    j = lax.broadcasted_iota(jnp.int32, (T, T), 1)
    pivots = jnp.sum(jnp.where(i == j, full, 0.0), axis=1, keepdims=True)
    unit = jnp.where(i > j, full, jnp.where(i == j, 1.0, 0.0))
    return unit * lax.rsqrt(pivots)

def solve_kernel(count_ref, gram_ref, steer_ref, out_ref, cov, rhs, inv):
    n = gram_ref.shape[0] // T
    scale = (BLOCK * count_ref[0]).astype(jnp.float32)
    i = lax.broadcasted_iota(jnp.int32, cov.shape, 0)
    j = lax.broadcasted_iota(jnp.int32, cov.shape, 1)
    cov[...] = gram_ref[...] / scale + jnp.where(i == j, LOADING, 0.0)
    rhs[...] = steer_ref[...].astype(jnp.float32)
    for b in range(n):
        lo, hi = b * T, (b + 1) * T
        inv[b] = factor_inverse(cov[lo:hi, lo:hi])
        li = inv[b]
        y = mm(li, rhs[lo:hi, :], 1, 0)
        rhs[lo:hi, :] = y
        if b + 1 < n:
            panel = mm(cov[hi:, lo:hi], li, 1, 1)
            cov[hi:, lo:hi] = panel
            cov[hi:, hi:] = cov[hi:, hi:] - mm(panel, panel, 1, 1)
            rhs[hi:, :] = rhs[hi:, :] - mm(panel, y, 1, 0)
    for b in reversed(range(n)):
        lo, hi = b * T, (b + 1) * T
        y = rhs[lo:hi, :]
        if b + 1 < n:
            y = y - mm(cov[hi:, lo:hi], rhs[hi:, :], 0, 0)
        rhs[lo:hi, :] = mm(inv[b], y, 0, 0)
    solved = rhs[...]
    response = jnp.sum(steer_ref[...].astype(jnp.float32) * solved, axis=0, keepdims=True)
    out_ref[...] = (solved / response).astype(out_ref.dtype)

def solve(count, gram, steer):
    d, e = steer.shape
    return pl.pallas_call(
        solve_kernel,
        out_shape=jax.ShapeDtypeStruct((d, e), jnp.bfloat16),
        in_specs=[pl.BlockSpec(memory_space=pltpu.SMEM), pl.BlockSpec(memory_space=pltpu.VMEM), pl.BlockSpec(memory_space=pltpu.VMEM)],
        out_specs=pl.BlockSpec(memory_space=pltpu.VMEM),
        scratch_shapes=[pltpu.VMEM((d, d), jnp.float32), pltpu.VMEM((d, e), jnp.float32), pltpu.VMEM((d // T, T, T), jnp.float32)],
        name="solve",
    )(count, gram, steer)


def adapt(own_snaps, train_list, train_count, steering):
    own_bins, gate_total, channels = own_snaps.shape
    block_total = train_list.shape[1]
    chosen = selection(train_list, train_count)
    blocks = own_snaps.reshape(own_bins, block_total, gate_total // block_total, channels)
    masked = blocks * chosen.astype(own_snaps.dtype)[:, :, None, None]
    gram_sum = jnp.einsum("bnrd,bnre->bde", masked, blocks, preferred_element_type=jnp.float32)
    return solve(train_count, gram_sum[0], steering[0])[None]


def body(snapshots, steering, train_list, train_count):
    bin_total, gate_rows, channels = snapshots.shape
    own_bins = steering.shape[0]
    devices = bin_total // own_bins
    outgoing = snapshots.reshape(devices, own_bins, gate_rows, channels)
    arrived = lax.all_to_all(
        outgoing, ("range", "doppler"), split_axis=0, concat_axis=0, tiled=True
    )
    own_snaps = jnp.moveaxis(arrived, 1, 0).reshape(own_bins, devices * gate_rows, channels)
    weights = adapt(own_snaps, train_list, train_count, steering)
    return jnp.einsum(
        "bgd,bde->bge",
        snapshots,
        lax.all_gather(weights, ("range", "doppler"), axis=0, tiled=True),
        preferred_element_type=jnp.float32,
    ).astype(jnp.bfloat16)


def solution(mesh):
    placed = (
        P(None, ("range", "doppler"), None),
        P(("range", "doppler"), None, None),
        P(("range", "doppler"), None),
        P(("range", "doppler")),
    )
    return jax.shard_map(
        body,
        mesh=mesh,
        in_specs=placed,
        out_specs=P(None, ("range", "doppler"), None),
        check_vma=False,
    )
```

```python
import jax
import jax.numpy as jnp
from jax import lax
from jax.experimental import pallas as pl
from jax.experimental.pallas import tpu as pltpu
from jax.sharding import PartitionSpec as P

BLOCK = 128


LOADING = 0.1


def selection(train_list, train_count):
    block_total = train_list.shape[1]
    position = lax.broadcasted_iota(jnp.int32, (1, block_total, 1), 1)
    block_ids = lax.broadcasted_iota(jnp.int32, (1, 1, block_total), 2)
    matches = (train_list[:, :, None] == block_ids) & (position < train_count[:, None, None])
    return jnp.sum(matches.astype(jnp.int32), axis=1)


HI = lax.Precision.HIGHEST
T = 128
def mm(a, b, ca, cb):
    return lax.dot_general(a, b, (((ca,), (cb,)), ((), ())), precision=HI, preferred_element_type=jnp.float32)

def factor_inverse(block):
    lane = lax.broadcasted_iota(jnp.int32, (8, T), 1)
    sub = lax.broadcasted_iota(jnp.int32, (8, T), 0)
    rows = [block[8 * g:8 * g + 8, :] for g in range(T // 8)]
    for k in range(T):
        own, off = k // 8, k % 8
        row = rows[own][off:off + 1, :]
        inv = 1.0 / row[:, k:k + 1]
        scaled = jnp.where(lane[:1] == k, 1.0, row) * inv
        for g in range(own, T // 8):
            col = rows[g][:, k:k + 1]
            if g == own:
                if off == 7:
                    continue
                col = jnp.where(sub[:, :1] > off, col, 0.0)
                base = jnp.where((lane == k) & (sub > off), 0.0, rows[g])
            else:
                base = jnp.where(lane == k, 0.0, rows[g])
            rows[g] = base - col * scaled
    full = jnp.concatenate(rows, axis=0)
    i = lax.broadcasted_iota(jnp.int32, (T, T), 0)
    j = lax.broadcasted_iota(jnp.int32, (T, T), 1)
    pivots = jnp.sum(jnp.where(i == j, full, 0.0), axis=1, keepdims=True)
    unit = jnp.where(i > j, full, jnp.where(i == j, 1.0, 0.0))
    return unit * lax.rsqrt(pivots)

def solve_kernel(count_ref, gram_ref, steer_ref, out_ref, cov, rhs, inv):
    n = gram_ref.shape[0] // T
    scale = (BLOCK * count_ref[0]).astype(jnp.float32)
    i = lax.broadcasted_iota(jnp.int32, cov.shape, 0)
    j = lax.broadcasted_iota(jnp.int32, cov.shape, 1)
    cov[...] = gram_ref[...] / scale + jnp.where(i == j, LOADING, 0.0)
    rhs[...] = steer_ref[...].astype(jnp.float32)
    for b in range(n):
        lo, hi = b * T, (b + 1) * T
        inv[b] = factor_inverse(cov[lo:hi, lo:hi])
        li = inv[b]
        y = mm(li, rhs[lo:hi, :], 1, 0)
        rhs[lo:hi, :] = y
        if b + 1 < n:
            panel = mm(cov[hi:, lo:hi], li, 1, 1)
            cov[hi:, lo:hi] = panel
            cov[hi:, hi:] = cov[hi:, hi:] - mm(panel, panel, 1, 1)
            rhs[hi:, :] = rhs[hi:, :] - mm(panel, y, 1, 0)
    for b in reversed(range(n)):
        lo, hi = b * T, (b + 1) * T
        y = rhs[lo:hi, :]
        if b + 1 < n:
            y = y - mm(cov[hi:, lo:hi], rhs[hi:, :], 0, 0)
        rhs[lo:hi, :] = mm(inv[b], y, 0, 0)
    solved = rhs[...]
    response = jnp.sum(steer_ref[...].astype(jnp.float32) * solved, axis=0, keepdims=True)
    out_ref[...] = (solved / response).astype(out_ref.dtype)

def solve(count, gram, steer):
    d, e = steer.shape
    return pl.pallas_call(
        solve_kernel,
        out_shape=jax.ShapeDtypeStruct((d, e), jnp.bfloat16),
        in_specs=[pl.BlockSpec(memory_space=pltpu.SMEM), pl.BlockSpec(memory_space=pltpu.VMEM), pl.BlockSpec(memory_space=pltpu.VMEM)],
        out_specs=pl.BlockSpec(memory_space=pltpu.VMEM),
        scratch_shapes=[pltpu.VMEM((d, d), jnp.float32), pltpu.VMEM((d, e), jnp.float32), pltpu.VMEM((d // T, T, T), jnp.float32)],
        name="solve",
    )(count, gram, steer)


MESH = pl.DeviceIdType.MESH
SIDE = 4
ORDERS = (("x", "y", "z"), ("y", "z", "x"), ("z", "x", "y"))

def place():
    r, d = lax.axis_index("range"), lax.axis_index("doppler")
    return {"z": r // SIDE, "y": r % SIDE, "x": d // 2, "c": d % 2}

def device(at):
    return (at["z"] * SIDE + at["y"], at["x"] * 2 + at["c"])

def moved(at, axis, step):
    return {**at, axis: (at[axis] + step) % SIDE}

def twin(at):
    return {**at, "c": 1 - at["c"]}

def greet(at):
    barrier = pltpu.get_barrier_semaphore()
    friends = [moved(at, a, s) for a in "xyz" for s in (1, SIDE - 1)] + [twin(at)]
    for friend in friends:
        pl.semaphore_signal(barrier, inc=1, device_id=device(friend), device_id_type=MESH)
    pl.semaphore_wait(barrier, len(friends))

def gather_kernel(own_ref, all_ref, local_sem, send_sem, recv_sem, twin_send, twin_recv):
    at = place()
    rows = own_ref.shape[0] // 3
    half = rows // 2
    greet(at)

    def window(part, gathered, where, halves):
        lo, count = (part * rows, rows) if halves is None else (part * rows + halves * half, half)
        pick = tuple(slice(None) if a in gathered else where[a] for a in "zyx")
        return all_ref.at[pick + (where["c"], pl.ds(lo, count), slice(None))]

    pending = []
    def send(part, stage, kind, gathered, where, halves, target):
        ref = window(part, gathered, where, halves)
        copy = pltpu.make_async_remote_copy(
            src_ref=ref, dst_ref=ref, send_sem=send_sem.at[part, stage, kind], recv_sem=recv_sem.at[part, stage, kind],
            device_id=device(target), device_id_type=MESH)
        copy.start()
        pending.append(copy)
    def arrive(part, stage, kind, gathered, where, halves):
        ref = window(part, gathered, where, halves)
        pltpu.make_async_remote_copy(
            src_ref=ref, dst_ref=ref, send_sem=send_sem.at[part, stage, kind], recv_sem=recv_sem.at[part, stage, kind],
            device_id=device(at), device_id_type=MESH).wait_recv()
    shared = []
    def share(part, stage, kind, gathered, where, halves):
        ref = window(part, gathered, where, halves)
        copy = pltpu.make_async_remote_copy(
            src_ref=ref, dst_ref=ref, send_sem=twin_send.at[part, stage, kind], recv_sem=twin_recv.at[part, stage, kind],
            device_id=device(twin(at)), device_id_type=MESH)
        copy.start()
        shared.append((copy, part, stage, kind, gathered, where, halves))

    mine = all_ref.at[at["z"], at["y"], at["x"], at["c"]]
    copy = pltpu.make_async_copy(own_ref, mine, local_sem)
    copy.start()
    copy.wait()
    for part in range(3):
        share(part, 3, 0, (), at, None)
    for stage in range(3):
        for part in range(3):
            axis, gathered = ORDERS[part][stage], ORDERS[part][:stage]
            up, down = moved(at, axis, 1), moved(at, axis, SIDE - 1)
            send(part, stage, 0, gathered, at, 0, up)
            send(part, stage, 1, gathered, at, 1, down)
            send(part, stage, 2, gathered, at, 1, up)
            send(part, stage, 3, gathered, at, 0, down)
        for part in range(3):
            axis, gathered = ORDERS[part][stage], ORDERS[part][:stage]
            up, down = moved(at, axis, 1), moved(at, axis, SIDE - 1)
            arrive(part, stage, 0, gathered, down, 0)
            send(part, stage, 4, gathered, down, 0, up)
            share(part, stage, 0, gathered, down, 0)
            arrive(part, stage, 1, gathered, up, 1)
            send(part, stage, 5, gathered, up, 1, down)
            share(part, stage, 1, gathered, up, 1)
        for part in range(3):
            axis, gathered = ORDERS[part][stage], ORDERS[part][:stage]
            up, down, far = moved(at, axis, 1), moved(at, axis, SIDE - 1), moved(at, axis, 2)
            for kind, where, halves in ((2, down, 1), (3, up, 0), (4, far, 0), (5, far, 1)):
                arrive(part, stage, kind, gathered, where, halves)
                share(part, stage, kind, gathered, where, halves)
    for copy in pending:
        copy.wait_send()
    for copy, part, stage, kind, gathered, where, halves in shared:
        copy.wait_send()
        ref = window(part, gathered, twin(where), halves)
        pltpu.make_async_remote_copy(
            src_ref=ref, dst_ref=ref, send_sem=twin_send.at[part, stage, kind], recv_sem=twin_recv.at[part, stage, kind],
            device_id=device(twin(at)), device_id_type=MESH).wait_recv()

def gather(own):
    rows, columns = own.shape
    whole = pl.pallas_call(
        gather_kernel,
        out_shape=jax.ShapeDtypeStruct((SIDE, SIDE, SIDE, 2, rows, columns), own.dtype),
        in_specs=[pl.BlockSpec(memory_space=pltpu.VMEM)],
        out_specs=pl.BlockSpec(memory_space=pl.ANY),
        scratch_shapes=[pltpu.SemaphoreType.DMA, pltpu.SemaphoreType.DMA((3, 3, 6)), pltpu.SemaphoreType.DMA((3, 3, 6)),
                        pltpu.SemaphoreType.DMA((3, 4, 6)), pltpu.SemaphoreType.DMA((3, 4, 6))],
        compiler_params=pltpu.CompilerParams(collective_id=1, has_side_effects=True),
        name="gather",
    )(own)
    return whole.reshape(SIDE * SIDE * SIDE * 2, rows, columns)

def apply_kernel(snap_ref, weight_ref, out_ref):
    for b in range(snap_ref.shape[0]):
        out_ref[b] = jnp.dot(snap_ref[b], weight_ref[b], preferred_element_type=jnp.float32).astype(out_ref.dtype)

def beams(snapshots, weights, step=8):
    bins, gates, channels = snapshots.shape
    looks = weights.shape[2]
    return pl.pallas_call(
        apply_kernel,
        grid=(bins // step,),
        out_shape=jax.ShapeDtypeStruct((bins, gates, looks), jnp.bfloat16),
        in_specs=[pl.BlockSpec((step, gates, channels), lambda i: (i, 0, 0)), pl.BlockSpec((step, channels, looks), lambda i: (i, 0, 0))],
        out_specs=pl.BlockSpec((step, gates, looks), lambda i: (i, 0, 0)),
        name="beams",
    )(snapshots, weights)


def adapt(own_snaps, train_list, train_count, steering):
    own_bins, gate_total, channels = own_snaps.shape
    block_total = train_list.shape[1]
    chosen = selection(train_list, train_count)
    blocks = own_snaps.reshape(own_bins, block_total, gate_total // block_total, channels)
    masked = blocks * chosen.astype(own_snaps.dtype)[:, :, None, None]
    gram_sum = jnp.einsum("bnrd,bnre->bde", masked, blocks, preferred_element_type=jnp.float32)
    return solve(train_count, gram_sum[0], steering[0])[None]


def body(snapshots, steering, train_list, train_count):
    bin_total, gate_rows, channels = snapshots.shape
    own_bins = steering.shape[0]
    devices = bin_total // own_bins
    outgoing = snapshots.reshape(devices, own_bins, gate_rows, channels)
    arrived = lax.all_to_all(
        outgoing, ("range", "doppler"), split_axis=0, concat_axis=0, tiled=True
    )
    own_snaps = jnp.moveaxis(arrived, 1, 0).reshape(own_bins, devices * gate_rows, channels)
    weights = adapt(own_snaps, train_list, train_count, steering)
    return beams(snapshots, gather(weights[0]))


def solution(mesh):
    placed = (
        P(None, ("range", "doppler"), None),
        P(("range", "doppler"), None, None),
        P(("range", "doppler"), None),
        P(("range", "doppler")),
    )
    return jax.shard_map(
        body,
        mesh=mesh,
        in_specs=placed,
        out_specs=P(None, ("range", "doppler"), None),
        check_vma=False,
    )
```

```python
import jax
import jax.numpy as jnp
from jax import lax
from jax.experimental import pallas as pl
from jax.experimental.pallas import tpu as pltpu
from jax.sharding import PartitionSpec as P

BLOCK = 128
LOADING = 0.1


def selection(train_list, train_count):
    block_total = train_list.shape[1]
    position = lax.broadcasted_iota(jnp.int32, (1, block_total, 1), 1)
    block_ids = lax.broadcasted_iota(jnp.int32, (1, 1, block_total), 2)
    matches = (train_list[:, :, None] == block_ids) & (position < train_count[:, None, None])
    return jnp.sum(matches.astype(jnp.int32), axis=1)


HI = lax.Precision.HIGHEST
T = 128
def mm(a, b, ca, cb):
    return lax.dot_general(a, b, (((ca,), (cb,)), ((), ())), precision=HI, preferred_element_type=jnp.float32)

def factor_inverse(block):
    lane = lax.broadcasted_iota(jnp.int32, (8, T), 1)
    sub = lax.broadcasted_iota(jnp.int32, (8, T), 0)
    rows = [block[8 * g:8 * g + 8, :] for g in range(T // 8)]
    for k in range(T):
        own, off = k // 8, k % 8
        row = rows[own][off:off + 1, :]
        inv = 1.0 / row[:, k:k + 1]
        scaled = jnp.where(lane[:1] == k, 1.0, row) * inv
        for g in range(own, T // 8):
            col = rows[g][:, k:k + 1]
            if g == own:
                if off == 7:
                    continue
                col = jnp.where(sub[:, :1] > off, col, 0.0)
                base = jnp.where((lane == k) & (sub > off), 0.0, rows[g])
            else:
                base = jnp.where(lane == k, 0.0, rows[g])
            rows[g] = base - col * scaled
    full = jnp.concatenate(rows, axis=0)
    i = lax.broadcasted_iota(jnp.int32, (T, T), 0)
    j = lax.broadcasted_iota(jnp.int32, (T, T), 1)
    pivots = jnp.sum(jnp.where(i == j, full, 0.0), axis=1, keepdims=True)
    unit = jnp.where(i > j, full, jnp.where(i == j, 1.0, 0.0))
    return unit * lax.rsqrt(pivots)

def solve_kernel(count_ref, gram_ref, steer_ref, out_ref, cov, rhs, inv):
    n = cov.shape[0] // T
    scale = (BLOCK * count_ref[0]).astype(jnp.float32)
    i = lax.broadcasted_iota(jnp.int32, (T, T), 0)
    j = lax.broadcasted_iota(jnp.int32, (T, T), 1)
    tiles = unpack(gram_ref, pltpu.roll)
    for (r, c), tile in zip(((0, 0), (1, 0), (1, 1), (2, 0), (2, 1), (2, 2)), tiles):
        tile = tile / scale
        cov[r * T:(r + 1) * T, c * T:(c + 1) * T] = tile + jnp.where(i == j, LOADING, 0.0) if r == c else tile
    cov[T:2 * T, 2 * T:] = jnp.zeros((T, T), jnp.float32)
    rhs[...] = steer_ref[...].astype(jnp.float32)
    for b in range(n):
        lo, hi = b * T, (b + 1) * T
        inv[b] = factor_inverse(cov[lo:hi, lo:hi])
        li = inv[b]
        y = mm(li, rhs[lo:hi, :], 1, 0)
        rhs[lo:hi, :] = y
        if b + 1 < n:
            panel = mm(cov[hi:, lo:hi], li, 1, 1)
            cov[hi:, lo:hi] = panel
            cov[hi:, hi:] = cov[hi:, hi:] - mm(panel, panel, 1, 1)
            rhs[hi:, :] = rhs[hi:, :] - mm(panel, y, 1, 0)
    for b in reversed(range(n)):
        lo, hi = b * T, (b + 1) * T
        y = rhs[lo:hi, :]
        if b + 1 < n:
            y = y - mm(cov[hi:, lo:hi], rhs[hi:, :], 0, 0)
        rhs[lo:hi, :] = mm(inv[b], y, 0, 0)
    solved = rhs[...]
    response = jnp.sum(steer_ref[...].astype(jnp.float32) * solved, axis=0, keepdims=True)
    out_ref[...] = (solved / response).astype(out_ref.dtype)

def solve(count, gram, steer):
    d, e = steer.shape
    return pl.pallas_call(
        solve_kernel,
        out_shape=jax.ShapeDtypeStruct((d, e), jnp.bfloat16),
        in_specs=[pl.BlockSpec(memory_space=pltpu.SMEM), pl.BlockSpec(memory_space=pltpu.VMEM), pl.BlockSpec(memory_space=pltpu.VMEM)],
        out_specs=pl.BlockSpec(memory_space=pltpu.VMEM),
        scratch_shapes=[pltpu.VMEM((d, d), jnp.float32), pltpu.VMEM((d, e), jnp.float32), pltpu.VMEM((d // T, T, T), jnp.float32)],
        name="solve",
    )(count, gram, steer)


MESH = pl.DeviceIdType.MESH
SIDE = 4
ORDERS = (("x", "y", "z"), ("y", "z", "x"), ("z", "x", "y"))

def place():
    r, d = lax.axis_index("range"), lax.axis_index("doppler")
    return {"z": r // SIDE, "y": r % SIDE, "x": d // 2, "c": d % 2}

def device(at):
    return (at["z"] * SIDE + at["y"], at["x"] * 2 + at["c"])

def moved(at, axis, step):
    return {**at, axis: (at[axis] + step) % SIDE}

def twin(at):
    return {**at, "c": 1 - at["c"]}

def greet(at):
    barrier = pltpu.get_barrier_semaphore()
    friends = [moved(at, a, s) for a in "xyz" for s in (1, SIDE - 1)] + [twin(at)]
    for friend in friends:
        pl.semaphore_signal(barrier, inc=1, device_id=device(friend), device_id_type=MESH)
    pl.semaphore_wait(barrier, len(friends))

def gather_kernel(own_ref, all_ref, local_sem, send_sem, recv_sem, twin_send, twin_recv):
    at = place()
    rows = own_ref.shape[0] // 3
    half = rows // 2
    greet(at)

    def window(part, gathered, where, halves):
        lo, count = (part * rows, rows) if halves is None else (part * rows + halves * half, half)
        pick = tuple(slice(None) if a in gathered else where[a] for a in "zyx")
        return all_ref.at[pick + (where["c"], pl.ds(lo, count), slice(None))]

    pending = []
    def send(part, stage, kind, gathered, where, halves, target):
        ref = window(part, gathered, where, halves)
        copy = pltpu.make_async_remote_copy(
            src_ref=ref, dst_ref=ref, send_sem=send_sem.at[part, stage, kind], recv_sem=recv_sem.at[part, stage, kind],
            device_id=device(target), device_id_type=MESH)
        copy.start()
        pending.append(copy)
    def arrive(part, stage, kind, gathered, where, halves):
        ref = window(part, gathered, where, halves)
        pltpu.make_async_remote_copy(
            src_ref=ref, dst_ref=ref, send_sem=send_sem.at[part, stage, kind], recv_sem=recv_sem.at[part, stage, kind],
            device_id=device(at), device_id_type=MESH).wait_recv()
    shared = []
    def share(part, stage, kind, gathered, where, halves):
        ref = window(part, gathered, where, halves)
        copy = pltpu.make_async_remote_copy(
            src_ref=ref, dst_ref=ref, send_sem=twin_send.at[part, stage, kind], recv_sem=twin_recv.at[part, stage, kind],
            device_id=device(twin(at)), device_id_type=MESH)
        copy.start()
        shared.append((copy, part, stage, kind, gathered, where, halves))

    mine = all_ref.at[at["z"], at["y"], at["x"], at["c"]]
    copy = pltpu.make_async_copy(own_ref, mine, local_sem)
    copy.start()
    copy.wait()
    for part in range(3):
        share(part, 3, 0, (), at, None)
    for stage in range(3):
        for part in range(3):
            axis, gathered = ORDERS[part][stage], ORDERS[part][:stage]
            up, down = moved(at, axis, 1), moved(at, axis, SIDE - 1)
            send(part, stage, 0, gathered, at, 0, up)
            send(part, stage, 1, gathered, at, 1, down)
            send(part, stage, 2, gathered, at, 1, up)
            send(part, stage, 3, gathered, at, 0, down)
        for part in range(3):
            axis, gathered = ORDERS[part][stage], ORDERS[part][:stage]
            up, down = moved(at, axis, 1), moved(at, axis, SIDE - 1)
            arrive(part, stage, 0, gathered, down, 0)
            send(part, stage, 4, gathered, down, 0, up)
            share(part, stage, 0, gathered, down, 0)
            arrive(part, stage, 1, gathered, up, 1)
            send(part, stage, 5, gathered, up, 1, down)
            share(part, stage, 1, gathered, up, 1)
        for part in range(3):
            axis, gathered = ORDERS[part][stage], ORDERS[part][:stage]
            up, down, far = moved(at, axis, 1), moved(at, axis, SIDE - 1), moved(at, axis, 2)
            for kind, where, halves in ((2, down, 1), (3, up, 0), (4, far, 0), (5, far, 1)):
                arrive(part, stage, kind, gathered, where, halves)
                share(part, stage, kind, gathered, where, halves)
    for copy in pending:
        copy.wait_send()
    for copy, part, stage, kind, gathered, where, halves in shared:
        copy.wait_send()
        ref = window(part, gathered, twin(where), halves)
        pltpu.make_async_remote_copy(
            src_ref=ref, dst_ref=ref, send_sem=twin_send.at[part, stage, kind], recv_sem=twin_recv.at[part, stage, kind],
            device_id=device(twin(at)), device_id_type=MESH).wait_recv()

def gather(own):
    rows, columns = own.shape
    whole = pl.pallas_call(
        gather_kernel,
        out_shape=jax.ShapeDtypeStruct((SIDE, SIDE, SIDE, 2, rows, columns), own.dtype),
        in_specs=[pl.BlockSpec(memory_space=pltpu.VMEM)],
        out_specs=pl.BlockSpec(memory_space=pl.ANY),
        scratch_shapes=[pltpu.SemaphoreType.DMA, pltpu.SemaphoreType.DMA((3, 3, 6)), pltpu.SemaphoreType.DMA((3, 3, 6)),
                        pltpu.SemaphoreType.DMA((3, 4, 6)), pltpu.SemaphoreType.DMA((3, 4, 6))],
        compiler_params=pltpu.CompilerParams(collective_id=1, has_side_effects=True),
        name="gather",
    )(own)
    return whole.reshape(SIDE * SIDE * SIDE * 2, rows, columns)

def apply_kernel(snap_ref, weight_ref, out_ref):
    for b in range(snap_ref.shape[0]):
        out_ref[b] = jnp.dot(snap_ref[b], weight_ref[b], preferred_element_type=jnp.float32).astype(out_ref.dtype)

def beams(snapshots, weights, step=8):
    bins, gates, channels = snapshots.shape
    looks = weights.shape[2]
    return pl.pallas_call(
        apply_kernel,
        grid=(bins // step,),
        out_shape=jax.ShapeDtypeStruct((bins, gates, looks), jnp.bfloat16),
        in_specs=[pl.BlockSpec((step, gates, channels), lambda i: (i, 0, 0)), pl.BlockSpec((step, channels, looks), lambda i: (i, 0, 0))],
        out_specs=pl.BlockSpec((step, gates, looks), lambda i: (i, 0, 0)),
        name="beams",
    )(snapshots, weights)


HALF = 64
PACKED = 200
CUT = 104
TOP, LOW, ALL = (0, CUT), (CUT, PACKED - CUT), (0, PACKED)
REDUCE = (("z", "y", "x"), ("x", "z", "y"), ("y", "x", "z"))

def cross(a, b):
    return lax.dot_general(a, b, (((0,), (0,)), ((), ())), preferred_element_type=jnp.float32)

def packed_part(part, snaps):
    first, second, third = snaps[:, :T], snaps[:, T:2 * T], snaps[:, 2 * T:]
    i = lax.broadcasted_iota(jnp.int32, (HALF, T), 0)
    j = lax.broadcasted_iota(jnp.int32, (HALF, T), 1)
    if part == 2:
        both = cross(third, jnp.concatenate([first, third], axis=1))
        tile, square = both[:, :T], both[:, T:]
        turned = pltpu.roll(square[:HALF], HALF, axis=1)
        fold = jnp.where(j - HALF > i, turned, square[HALF:])
        ridge = jnp.where(j - HALF == i, turned, 0.0)
    else:
        lo = part * HALF
        lower = cross(first, first)[lo:lo + HALF]
        if part == 0:
            both = cross(second, snaps[:, :2 * T])
            tile, upper = both[:, :T], both[lo:lo + HALF, T:]
        else:
            both = cross(second, snaps[:, T:])
            tile, upper = both[:, T:], both[lo:lo + HALF, :T]
        fold = jnp.where(j <= i + lo, lower, upper)
        ridge = jnp.where(j == i + lo, upper, 0.0)
    return tile, fold, jnp.broadcast_to(jnp.sum(ridge, axis=0, keepdims=True), (8, T))

def unpack(packed, roll):
    i = lax.broadcasted_iota(jnp.int32, (T, T), 0)
    j = lax.broadcasted_iota(jnp.int32, (T, T), 1)
    fold = jnp.concatenate([packed[0, T:T + HALF], packed[1, T:T + HALF]], axis=0)
    ridge = packed[0, PACKED - 8:PACKED - 7] + packed[1, PACKED - 8:PACKED - 7]
    t00 = jnp.where(j <= i, fold, fold.T)
    t11 = jnp.where(j > i, fold, jnp.where(i == j, ridge, fold.T))
    low = packed[2, T:T + HALF]
    mixed = jnp.concatenate([roll(low, HALF, 1), low], axis=0)
    ridge = roll(packed[2, PACKED - 8:], HALF, 1)[:1]
    keep = ((i < HALF) & (j < HALF) & (j > i)) | ((i >= HALF) & (j <= i))
    t22 = jnp.where((i == j) & (i < HALF), ridge, jnp.where(keep, mixed, mixed.T))
    return t00, packed[0, :T], t11, packed[2, :T], packed[1, :T].T, t22

def reduce_kernel(snap_ref, chosen_ref, out_ref, own, other, marks, grams, far1, down1, up1, far2, down2, up2, far3, down3, up3,
                  own_sem, twin_send, twin_recv, mark_send, mark_recv, send1, recv1, send2, recv2):
    at = place()
    greet(at)
    twin_at = twin(at)
    me = ((at["z"] * SIDE + at["y"]) * SIDE + at["x"]) * 2
    far = (far1, far2, far3)
    down_in = (down1, down2, down3)
    up_in = (up1, up2, up3)

    def turn(axis, step):
        return (at[axis] + step) % SIDE

    def own_copy(z):
        return pltpu.make_async_copy(snap_ref.at[z, :, :, at["c"]], own.at[z], own_sem.at[z])
    def twin_copy(z):
        return pltpu.make_async_remote_copy(
            src_ref=snap_ref.at[z, :, :, twin_at["c"]], dst_ref=other.at[z], send_sem=twin_send.at[z], recv_sem=twin_recv.at[z],
            device_id=device(twin_at), device_id_type=MESH)
    order = [turn("z", s) for s in (2, 1, 3, 0)]

    def mark_copy(stage, kind):
        axis = "xyz"[stage]
        where = moved(at, axis, SIDE - 1) if kind == 2 else at
        ref = marks.at[(where["z"], where["y"], where["x"])[:SIDE - 1 - stage]]
        target = moved(at, axis, SIDE - 1 if kind == 1 else 1)
        return pltpu.make_async_remote_copy(
            src_ref=ref, dst_ref=ref, send_sem=mark_send.at[stage, kind], recv_sem=mark_recv.at[stage, kind],
            device_id=device(target), device_id_type=MESH)
    for z in order:
        twin_copy(z).start()
        own_copy(z).start()
    marks[at["z"], at["y"], at["x"]] = chosen_ref[...]
    for stage in range(3):
        mark_copy(stage, 0).start()
        mark_copy(stage, 1).start()
        mark_copy(stage, 0).wait_recv()
        mark_copy(stage, 2).start()
        mark_copy(stage, 1).wait_recv()
        mark_copy(stage, 2).wait_recv()
    for stage in range(3):
        for kind in range(3):
            mark_copy(stage, kind).wait_send()

    lane = lax.broadcasted_iota(jnp.int32, (1, T), 1)
    def ready(z):
        own_copy(z).wait()
        twin_copy(z).wait_recv()
        def mask(n, carry):
            y, x = n // SIDE, n % SIDE
            row = marks[z, y, x][:1]
            for ref, block in ((own, me + at["c"]), (other, me + twin_at["c"])):
                keep = jnp.sum(jnp.where(lane == block, row, 0.0), axis=1, keepdims=True)
                ref[z, y, x] = (ref[z, y, x].astype(jnp.float32) * keep).astype(jnp.bfloat16)
            return carry
        lax.fori_loop(0, SIDE * SIDE, mask, 0)

    def compute(part, i3, i2):
        names = REDUCE[part]
        def one(i1, carry):
            where = dict(zip(names, (i3, i2, i1)))
            spot = (where["z"], where["y"], where["x"])
            snaps = jnp.concatenate([own[spot], other[spot]], axis=0)
            tile, fold, ridge = packed_part(part, snaps)
            grams[part, i3, i2, i1, 0:T] = tile
            grams[part, i3, i2, i1, T:T + HALF] = fold
            grams[part, i3, i2, i1, T + HALF:PACKED] = ridge
            return carry
        lax.fori_loop(0, SIDE, one, 0)

    KIND = (
        (2, TOP, "far", 1), (2, LOW, "far", SIDE - 1), (1, LOW, "near", 1),
        (SIDE - 1, TOP, "near", SIDE - 1), (1, TOP, "near", 1), (SIDE - 1, LOW, "near", SIDE - 1),
    )
    def hop(part, stage, kind, chunk=None):
        step, (lo, count), slot, way = KIND[kind]
        names = REDUCE[part]
        prefix = tuple(at[a] for a in names[:stage])
        tail = () if chunk is None else (chunk,)
        rows = (slice(None),) * (2 - stage - len(tail)) + (pl.ds(lo, count), slice(None))
        src = grams.at[(part,) + prefix + (turn(names[stage], step),) + tail + rows]
        box = far[stage] if slot == "far" else (down_in[stage] if way == 1 else up_in[stage])
        dst = box.at[(part,) + tail + rows]
        if chunk is None:
            ss, rs = send2.at[part, stage - 1, kind], recv2.at[part, stage - 1, kind]
        else:
            ss, rs = send1.at[part, kind, chunk], recv1.at[part, kind, chunk]
        return pltpu.make_async_remote_copy(
            src_ref=src, dst_ref=dst, send_sem=ss, recv_sem=rs,
            device_id=device(moved(at, names[stage], way)), device_id_type=MESH)

    def add_far(part, stage, kind, chunk=None):
        names = REDUCE[part]
        prefix = tuple(at[a] for a in names[:stage])
        tail = () if chunk is None else (chunk,)
        step, (lo, count) = (1, TOP) if kind == 0 else (SIDE - 1, LOW)
        whole = (slice(None),) * (2 - stage - len(tail)) + (slice(lo, lo + count), slice(None))
        spot = (part,) + prefix + (turn(names[stage], step),) + tail + whole
        grams[spot] = grams[spot] + far[stage][(part,) + tail + whole]

    def add_near(part, stage, chunk=None):
        names = REDUCE[part]
        tail = () if chunk is None else (chunk,)
        spot = (part,) + tuple(at[a] for a in names[:stage + 1]) + tail
        got = (part,) + tail
        grams[spot] = grams[spot] + down_in[stage][got] + up_in[stage][got]

    def second(part, q):
        return (at[REDUCE[part][1]] + 6 - q) % SIDE

    def loop(body):
        def run(q, carry):
            body(q)
            return carry
        lax.fori_loop(0, SIDE, run, 0)

    def far_out(part):
        def body(q):
            compute(part, turn(REDUCE[part][0], 2), second(part, q))
            hop(part, 0, 0, second(part, q)).start()
            hop(part, 0, 1, second(part, q)).start()
        loop(body)

    ready(order[0])
    far_out(0)
    for z in order[1:]:
        ready(z)
    far_out(1)
    far_out(2)

    def near_out(q):
        for part in range(3):
            for step, kind in ((1, 2), (SIDE - 1, 3)):
                compute(part, turn(REDUCE[part][0], step), second(part, q))
                hop(part, 0, kind, second(part, q)).start()
    loop(near_out)

    def relay(q):
        for part in range(3):
            compute(part, at[REDUCE[part][0]], second(part, q))
        for part in range(3):
            chunk = second(part, q)
            for kind in (0, 1):
                hop(part, 0, kind, chunk).wait_recv()
                add_far(part, 0, kind, chunk)
                hop(part, 0, kind + 4, chunk).start()
    loop(relay)

    for q in range(SIDE):
        for part in range(3):
            chunk = second(part, q)
            for kind in (2, 3, 4, 5):
                hop(part, 0, kind, chunk).wait_recv()
            add_near(part, 0, chunk)
            for kind in ((0, 1), (2,), (), (3,))[q]:
                hop(part, 1, kind).start()
    for stage in (1, 2):
        for part in range(3):
            for kind in (0, 1):
                hop(part, stage, kind).wait_recv()
                add_far(part, stage, kind)
                hop(part, stage, kind + 4).start()
        for part in range(3):
            for kind in (2, 3, 4, 5):
                hop(part, stage, kind).wait_recv()
            add_near(part, stage)
            if stage == 1:
                for kind in range(4):
                    hop(part, 2, kind).start()
    for part in range(3):
        out_ref[part] = grams[(part,) + tuple(at[a] for a in REDUCE[part])]

    for z in order:
        twin_copy(z).wait_send()
    def drain(q):
        for part in range(3):
            for kind in range(6):
                hop(part, 0, kind, q).wait_send()
    loop(drain)
    for part in range(3):
        for stage in (1, 2):
            for kind in range(6):
                hop(part, stage, kind).wait_send()

def reduce_grams(snapshots, chosen):
    bins, gates, channels = snapshots.shape
    split = snapshots.reshape(SIDE, SIDE, SIDE, 2, gates, channels)
    f32, sem = jnp.float32, pltpu.SemaphoreType.DMA
    boxes = [pltpu.VMEM((3,) + (SIDE,) * n + (PACKED, T), f32) for n in (2, 2, 2, 1, 1, 1, 0, 0, 0)]
    return pl.pallas_call(
        reduce_kernel,
        out_shape=jax.ShapeDtypeStruct((3, PACKED, T), f32),
        in_specs=[pl.BlockSpec(memory_space=pl.ANY), pl.BlockSpec(memory_space=pltpu.VMEM)],
        out_specs=pl.BlockSpec(memory_space=pltpu.VMEM),
        scratch_shapes=[
            pltpu.VMEM((SIDE, SIDE, SIDE, gates, channels), jnp.bfloat16), pltpu.VMEM((SIDE, SIDE, SIDE, gates, channels), jnp.bfloat16),
            pltpu.VMEM((SIDE, SIDE, SIDE, 8, T), f32), pltpu.VMEM((3, SIDE, SIDE, SIDE, PACKED, T), f32), *boxes,
            sem((SIDE,)), sem((SIDE,)), sem((SIDE,)), sem((3, 3)), sem((3, 3)),
            sem((3, 6, SIDE)), sem((3, 6, SIDE)), sem((3, 2, 6)), sem((3, 2, 6)),
        ],
        compiler_params=pltpu.CompilerParams(collective_id=2, has_side_effects=True, vmem_limit_bytes=67000000),
        name="reduce_grams",
    )(split, chosen)


def body(snapshots, steering, train_list, train_count):
    chosen = selection(train_list, train_count).astype(jnp.float32)
    packed = reduce_grams(snapshots, jnp.broadcast_to(chosen, (8, BLOCK)))
    weights = solve(train_count, packed, steering[0])
    return beams(snapshots, gather(weights))


def solution(mesh):
    placed = (
        P(None, ("range", "doppler"), None),
        P(("range", "doppler"), None, None),
        P(("range", "doppler"), None),
        P(("range", "doppler")),
    )
    return jax.shard_map(
        body,
        mesh=mesh,
        in_specs=placed,
        out_specs=P(None, ("range", "doppler"), None),
        check_vma=False,
    )
```

```python
import jax
import jax.numpy as jnp
from jax import lax
from jax.experimental import pallas as pl
from jax.experimental.pallas import tpu as pltpu
from jax.sharding import PartitionSpec as P

BLOCK = 128
LOADING = 0.1


def selection(train_list, train_count):
    block_total = train_list.shape[1]
    position = lax.broadcasted_iota(jnp.int32, (1, block_total, 1), 1)
    block_ids = lax.broadcasted_iota(jnp.int32, (1, 1, block_total), 2)
    matches = (train_list[:, :, None] == block_ids) & (position < train_count[:, None, None])
    return jnp.sum(matches.astype(jnp.int32), axis=1)


HI = lax.Precision.HIGHEST
T = BLOCK
def mm(a, b, ca, cb):
    return lax.dot_general(a, b, (((ca,), (cb,)), ((), ())), precision=HI, preferred_element_type=jnp.float32)

def factor_inverse(block):
    lane = lax.broadcasted_iota(jnp.int32, (8, T), 1)
    sub = lax.broadcasted_iota(jnp.int32, (8, T), 0)
    rows = [block[8 * g:8 * g + 8, :] for g in range(T // 8)]
    for k in range(T):
        own, off = k // 8, k % 8
        row = rows[own][off:off + 1, :]
        inv = 1.0 / row[:, k:k + 1]
        scaled = jnp.where(lane[:1] == k, 1.0, row) * inv
        for g in range(own, T // 8):
            col = rows[g][:, k:k + 1]
            if g == own:
                if off == 7:
                    continue
                col = jnp.where(sub[:, :1] > off, col, 0.0)
                base = jnp.where((lane == k) & (sub > off), 0.0, rows[g])
            else:
                base = jnp.where(lane == k, 0.0, rows[g])
            rows[g] = base - col * scaled
    full = jnp.concatenate(rows, axis=0)
    i = lax.broadcasted_iota(jnp.int32, (T, T), 0)
    j = lax.broadcasted_iota(jnp.int32, (T, T), 1)
    pivots = jnp.sum(jnp.where(i == j, full, 0.0), axis=1, keepdims=True)
    unit = jnp.where(i > j, full, jnp.where(i == j, 1.0, 0.0))
    return unit * lax.rsqrt(pivots)


MESH = pl.DeviceIdType.MESH
SIDE = 4
ORDERS = (("x", "y", "z"), ("y", "z", "x"), ("z", "x", "y"))

def place():
    r, d = lax.axis_index("range"), lax.axis_index("doppler")
    return {"z": r // SIDE, "y": r % SIDE, "x": d // 2, "c": d % 2}

def device(at):
    return (at["z"] * SIDE + at["y"], at["x"] * 2 + at["c"])

def moved(at, axis, step):
    return {**at, axis: (at[axis] + step) % SIDE}

def twin(at):
    return {**at, "c": 1 - at["c"]}

def greet(at):
    barrier = pltpu.get_barrier_semaphore()
    friends = [moved(at, a, s) for a in "xyz" for s in (1, SIDE - 1)] + [twin(at)]
    for friend in friends:
        pl.semaphore_signal(barrier, inc=1, device_id=device(friend), device_id_type=MESH)
    pl.semaphore_wait(barrier, len(friends))

HALF = 64
PACKED = 200
CUT = 104
TOP, LOW, ALL = (0, CUT), (CUT, PACKED - CUT), (0, PACKED)
REDUCE = (("z", "y", "x"), ("x", "z", "y"), ("y", "x", "z"))

def cross(a, b):
    return lax.dot_general(a, b, (((0,), (0,)), ((), ())), preferred_element_type=jnp.float32)

def packed_part(part, snaps):
    first, second, third = snaps[:, :T], snaps[:, T:2 * T], snaps[:, 2 * T:]
    i = lax.broadcasted_iota(jnp.int32, (HALF, T), 0)
    j = lax.broadcasted_iota(jnp.int32, (HALF, T), 1)
    if part == 2:
        both = cross(third, jnp.concatenate([first, third], axis=1))
        tile, square = both[:, :T], both[:, T:]
        turned = pltpu.roll(square[:HALF], HALF, axis=1)
        fold = jnp.where(j - HALF > i, turned, square[HALF:])
        ridge = jnp.where(j - HALF == i, turned, 0.0)
    else:
        lo = part * HALF
        lower = cross(first, first)[lo:lo + HALF]
        if part == 0:
            both = cross(second, snaps[:, :2 * T])
            tile, upper = both[:, :T], both[lo:lo + HALF, T:]
        else:
            both = cross(second, snaps[:, T:])
            tile, upper = both[:, T:], both[lo:lo + HALF, :T]
        fold = jnp.where(j <= i + lo, lower, upper)
        ridge = jnp.where(j == i + lo, upper, 0.0)
    return tile, fold, jnp.broadcast_to(jnp.sum(ridge, axis=0, keepdims=True), (8, T))

def unpack(packed, roll):
    i = lax.broadcasted_iota(jnp.int32, (T, T), 0)
    j = lax.broadcasted_iota(jnp.int32, (T, T), 1)
    fold = jnp.concatenate([packed[0, T:T + HALF], packed[1, T:T + HALF]], axis=0)
    ridge = packed[0, PACKED - 8:PACKED - 7] + packed[1, PACKED - 8:PACKED - 7]
    t00 = jnp.where(j <= i, fold, fold.T)
    t11 = jnp.where(j > i, fold, jnp.where(i == j, ridge, fold.T))
    low = packed[2, T:T + HALF]
    mixed = jnp.concatenate([roll(low, HALF, 1), low], axis=0)
    ridge = roll(packed[2, PACKED - 8:], HALF, 1)[:1]
    keep = ((i < HALF) & (j < HALF) & (j > i)) | ((i >= HALF) & (j <= i))
    t22 = jnp.where((i == j) & (i < HALF), ridge, jnp.where(keep, mixed, mixed.T))
    return t00, packed[0, :T], t11, packed[2, :T], packed[1, :T].T, t22

def reduce_phase(at, snap_ref, chosen_ref, out_ref, go, own, other, marks, grams, far1, down1, up1, far2, down2, up2, far3, down3, up3,
                  own_sem, twin_send, twin_recv, mark_send, mark_recv, send1, recv1, send2, recv2):
    twin_at = twin(at)
    me = ((at["z"] * SIDE + at["y"]) * SIDE + at["x"]) * 2
    far = (far1, far2, far3)
    down_in = (down1, down2, down3)
    up_in = (up1, up2, up3)

    def turn(axis, step):
        return (at[axis] + step) % SIDE

    def own_copy(z):
        return pltpu.make_async_copy(snap_ref.at[z, :, :, at["c"]], own.at[z], own_sem.at[z])
    def twin_copy(z):
        return pltpu.make_async_remote_copy(
            src_ref=snap_ref.at[z, :, :, twin_at["c"]], dst_ref=other.at[z], send_sem=twin_send.at[z], recv_sem=twin_recv.at[z],
            device_id=device(twin_at), device_id_type=MESH)
    order = [turn("z", s) for s in (2, 1, 3, 0)]

    def mark_copy(stage, kind):
        axis = "xyz"[stage]
        where = moved(at, axis, SIDE - 1) if kind == 2 else at
        ref = marks.at[(where["z"], where["y"], where["x"])[:SIDE - 1 - stage]]
        target = moved(at, axis, SIDE - 1 if kind == 1 else 1)
        return pltpu.make_async_remote_copy(
            src_ref=ref, dst_ref=ref, send_sem=mark_send.at[stage, kind], recv_sem=mark_recv.at[stage, kind],
            device_id=device(target), device_id_type=MESH)
    for z in order:
        twin_copy(z).start()
        own_copy(z).start()
    marks[at["z"], at["y"], at["x"]] = chosen_ref[...]
    for stage in range(3):
        mark_copy(stage, 0).start()
        mark_copy(stage, 1).start()
        mark_copy(stage, 0).wait_recv()
        mark_copy(stage, 2).start()
        mark_copy(stage, 1).wait_recv()
        mark_copy(stage, 2).wait_recv()
    for stage in range(3):
        for kind in range(3):
            mark_copy(stage, kind).wait_send()

    lane = lax.broadcasted_iota(jnp.int32, (1, T), 1)
    def ready(z):
        own_copy(z).wait()
        twin_copy(z).wait_recv()
        def mask(n, carry):
            y, x = n // SIDE, n % SIDE
            row = marks[z, y, x][:1]
            for ref, block in ((own, me + at["c"]), (other, me + twin_at["c"])):
                keep = jnp.sum(jnp.where(lane == block, row, 0.0), axis=1, keepdims=True)
                ref[z, y, x] = (ref[z, y, x].astype(jnp.float32) * keep).astype(jnp.bfloat16)
            return carry
        lax.fori_loop(0, SIDE * SIDE, mask, 0, unroll=4)

    def compute(part, i3, i2):
        names = REDUCE[part]
        def one(i1, carry):
            where = dict(zip(names, (i3, i2, i1)))
            spot = (where["z"], where["y"], where["x"])
            snaps = jnp.concatenate([own[spot], other[spot]], axis=0)
            tile, fold, ridge = packed_part(part, snaps)
            grams[part, i3, i2, i1, 0:T] = tile
            grams[part, i3, i2, i1, T:T + HALF] = fold
            grams[part, i3, i2, i1, T + HALF:PACKED] = ridge
            return carry
        lax.fori_loop(0, SIDE, one, 0, unroll=True)

    KIND = (
        (2, TOP, "far", 1), (2, LOW, "far", SIDE - 1), (1, LOW, "near", 1),
        (SIDE - 1, TOP, "near", SIDE - 1), (1, TOP, "near", 1), (SIDE - 1, LOW, "near", SIDE - 1),
    )
    def hop(part, stage, kind, chunk=None):
        step, (lo, count), slot, way = KIND[kind]
        names = REDUCE[part]
        prefix = tuple(at[a] for a in names[:stage])
        tail = () if chunk is None else (chunk,)
        rows = (slice(None),) * (2 - stage - len(tail)) + (pl.ds(lo, count), slice(None))
        src = grams.at[(part,) + prefix + (turn(names[stage], step),) + tail + rows]
        box = far[stage] if slot == "far" else (down_in[stage] if way == 1 else up_in[stage])
        dst = box.at[(part,) + tail + rows]
        if chunk is None:
            ss, rs = send2.at[part, stage - 1, kind], recv2.at[part, stage - 1, kind]
        else:
            ss, rs = send1.at[part, kind, chunk], recv1.at[part, kind, chunk]
        return pltpu.make_async_remote_copy(
            src_ref=src, dst_ref=dst, send_sem=ss, recv_sem=rs,
            device_id=device(moved(at, names[stage], way)), device_id_type=MESH)

    def add_far(part, stage, kind, chunk=None):
        names = REDUCE[part]
        prefix = tuple(at[a] for a in names[:stage])
        tail = () if chunk is None else (chunk,)
        step, (lo, count) = (1, TOP) if kind == 0 else (SIDE - 1, LOW)
        whole = (slice(None),) * (2 - stage - len(tail)) + (slice(lo, lo + count), slice(None))
        spot = (part,) + prefix + (turn(names[stage], step),) + tail + whole
        grams[spot] = grams[spot] + far[stage][(part,) + tail + whole]

    def add_near(part, stage, chunk=None):
        names = REDUCE[part]
        tail = () if chunk is None else (chunk,)
        spot = (part,) + tuple(at[a] for a in names[:stage + 1]) + tail
        got = (part,) + tail
        grams[spot] = grams[spot] + down_in[stage][got] + up_in[stage][got]

    def second(part, q):
        return (at[REDUCE[part][1]] + 6 - q) % SIDE

    def loop(body):
        def run(q, carry):
            body(q)
            return carry
        lax.fori_loop(0, SIDE, run, 0)

    leads = at["c"] == 0

    def compute_first(part, i3, i2):
        pl.when(leads)(lambda: compute(part, i3, i2))

    def far_out(part):
        def body(q):
            compute_first(part, turn(REDUCE[part][0], 2), second(part, q))
            hop(part, 0, 0, second(part, q)).start()
            hop(part, 0, 1, second(part, q)).start()
        loop(body)

    ready(order[0])
    pl.when(leads)(lambda: far_out(0))
    for z in order[1:]:
        ready(z)

    @pl.when(jnp.logical_not(leads))
    def _():
        for part in range(3):
            def every(n, carry):
                compute(part, n // SIDE, n % SIDE)
                return carry
            lax.fori_loop(0, SIDE * SIDE, every, 0)
        pl.semaphore_wait(go, 1)
        far_out(0)

    far_out(1)
    far_out(2)

    def near_out(q):
        for part in range(3):
            for step, kind in ((1, 2), (SIDE - 1, 3)):
                compute_first(part, turn(REDUCE[part][0], step), second(part, q))
                hop(part, 0, kind, second(part, q)).start()
    loop(near_out)

    def relay(q):
        for part in range(3):
            compute_first(part, at[REDUCE[part][0]], second(part, q))
        for part in range(3):
            chunk = second(part, q)
            for kind in (0, 1):
                hop(part, 0, kind, chunk).wait_recv()
                add_far(part, 0, kind, chunk)
                hop(part, 0, kind + 4, chunk).start()
    loop(relay)

    for q in range(SIDE):
        for part in range(3):
            chunk = second(part, q)
            for kind in (2, 3, 4, 5):
                hop(part, 0, kind, chunk).wait_recv()
            add_near(part, 0, chunk)
            for kind in ((0, 1), (2,), (), (3,))[q]:
                hop(part, 1, kind).start()
    @pl.when(leads)
    def _():
        pl.semaphore_signal(go, inc=1, device_id=device(twin_at), device_id_type=MESH)

    for stage in (1, 2):
        for part in range(3):
            for kind in (0, 1):
                hop(part, stage, kind).wait_recv()
                add_far(part, stage, kind)
                hop(part, stage, kind + 4).start()
        for part in range(3):
            for kind in (2, 3, 4, 5):
                hop(part, stage, kind).wait_recv()
            add_near(part, stage)
            if stage == 1:
                for kind in range(4):
                    hop(part, 2, kind).start()
    for part in range(3):
        out_ref[part] = grams[(part,) + tuple(at[a] for a in REDUCE[part])]

    for z in order:
        twin_copy(z).wait_send()
    def drain(q):
        for part in range(3):
            for kind in range(6):
                hop(part, 0, kind, q).wait_send()
    loop(drain)
    for part in range(3):
        for stage in (1, 2):
            for kind in range(6):
                hop(part, stage, kind).wait_send()


def solve_phase(count_ref, packed, steer_ref, out_ref, diag, cov, rhs, inv):
    n = cov.shape[0] // T
    scale = (BLOCK * count_ref[0]).astype(jnp.float32)
    i = lax.broadcasted_iota(jnp.int32, (T, T), 0)
    j = lax.broadcasted_iota(jnp.int32, (T, T), 1)
    tiles = unpack(packed, pltpu.roll)
    for (r, c), tile in zip(((0, 0), (1, 0), (1, 1), (2, 0), (2, 1), (2, 2)), tiles):
        tile = tile / scale
        if r == c:
            diag[r] = tile + jnp.where(i == j, LOADING, 0.0)
        else:
            cov[r * T:(r + 1) * T, c * T:(c + 1) * T] = tile
    rhs[...] = steer_ref[...].astype(jnp.float32)

    def forward(b, carry):
        inv[b] = factor_inverse(diag[b])
        for which in range(n):
            def update(b=which):
                lo, hi = b * T, (b + 1) * T
                li = inv[b]
                y = mm(li, rhs[lo:hi, :], 1, 0)
                rhs[lo:hi, :] = y
                if b + 1 < n:
                    panel = mm(cov[hi:, lo:hi], li, 1, 1)
                    cov[hi:, lo:hi] = panel
                    diag[b + 1] = diag[b + 1] - mm(panel[:T], panel[:T], 1, 1)
                    rhs[hi:, :] = rhs[hi:, :] - mm(panel, y, 1, 0)
                if b + 2 < n:
                    diag[b + 2] = diag[b + 2] - mm(panel[T:], panel[T:], 1, 1)
                    cov[hi + T:, hi:hi + T] = cov[hi + T:, hi:hi + T] - mm(panel[T:], panel[:T], 1, 1)
            pl.when(b == which)(update)
        return carry
    lax.fori_loop(0, n, forward, 0)
    for b in reversed(range(n)):
        lo, hi = b * T, (b + 1) * T
        y = rhs[lo:hi, :]
        if b + 1 < n:
            y = y - mm(cov[hi:, lo:hi], rhs[hi:, :], 0, 0)
        rhs[lo:hi, :] = mm(inv[b], y, 0, 0)
    solved = rhs[...]
    response = jnp.sum(steer_ref[...].astype(jnp.float32) * solved, axis=0, keepdims=True)
    out_ref[...] = (solved / response).astype(out_ref.dtype)


def gather_phase(at, own_ref, all_ref, local_sem, send_sem, recv_sem, twin_send, twin_recv):
    rows = own_ref.shape[0] // 3
    half = rows // 2

    def window(part, gathered, where, halves):
        lo, count = (part * rows, rows) if halves is None else (part * rows + halves * half, half)
        pick = tuple(slice(None) if a in gathered else where[a] for a in "zyx")
        return all_ref.at[pick + (where["c"], pl.ds(lo, count), slice(None))]

    pending = []
    def send(part, stage, kind, gathered, where, halves, target):
        ref = window(part, gathered, where, halves)
        copy = pltpu.make_async_remote_copy(
            src_ref=ref, dst_ref=ref, send_sem=send_sem.at[part, stage, kind], recv_sem=recv_sem.at[part, stage, kind],
            device_id=device(target), device_id_type=MESH)
        copy.start()
        pending.append(copy)
    def arrive(part, stage, kind, gathered, where, halves):
        ref = window(part, gathered, where, halves)
        pltpu.make_async_remote_copy(
            src_ref=ref, dst_ref=ref, send_sem=send_sem.at[part, stage, kind], recv_sem=recv_sem.at[part, stage, kind],
            device_id=device(at), device_id_type=MESH).wait_recv()
    shared = []
    def share(part, stage, kind, gathered, where, halves):
        ref = window(part, gathered, where, halves)
        copy = pltpu.make_async_remote_copy(
            src_ref=ref, dst_ref=ref, send_sem=twin_send.at[part, stage, kind], recv_sem=twin_recv.at[part, stage, kind],
            device_id=device(twin(at)), device_id_type=MESH)
        copy.start()
        shared.append((copy, part, stage, kind, gathered, where, halves))

    mine = all_ref.at[at["z"], at["y"], at["x"], at["c"]]
    copy = pltpu.make_async_copy(own_ref, mine, local_sem)
    copy.start()
    copy.wait()
    for part in range(3):
        share(part, 3, 0, (), at, None)
    for stage in range(3):
        for part in range(3):
            axis, gathered = ORDERS[part][stage], ORDERS[part][:stage]
            up, down = moved(at, axis, 1), moved(at, axis, SIDE - 1)
            send(part, stage, 0, gathered, at, 0, up)
            send(part, stage, 1, gathered, at, 1, down)
            send(part, stage, 2, gathered, at, 1, up)
            send(part, stage, 3, gathered, at, 0, down)
        for part in range(3):
            axis, gathered = ORDERS[part][stage], ORDERS[part][:stage]
            up, down = moved(at, axis, 1), moved(at, axis, SIDE - 1)
            arrive(part, stage, 0, gathered, down, 0)
            send(part, stage, 4, gathered, down, 0, up)
            share(part, stage, 0, gathered, down, 0)
            arrive(part, stage, 1, gathered, up, 1)
            send(part, stage, 5, gathered, up, 1, down)
            share(part, stage, 1, gathered, up, 1)
        for part in range(3):
            axis, gathered = ORDERS[part][stage], ORDERS[part][:stage]
            up, down, far = moved(at, axis, 1), moved(at, axis, SIDE - 1), moved(at, axis, 2)
            for kind, where, halves in ((2, down, 1), (3, up, 0), (4, far, 0), (5, far, 1)):
                arrive(part, stage, kind, gathered, where, halves)
                share(part, stage, kind, gathered, where, halves)
    for copy in pending:
        copy.wait_send()
    for copy, part, stage, kind, gathered, where, halves in shared:
        copy.wait_send()
        ref = window(part, gathered, twin(where), halves)
        pltpu.make_async_remote_copy(
            src_ref=ref, dst_ref=ref, send_sem=twin_send.at[part, stage, kind], recv_sem=twin_recv.at[part, stage, kind],
            device_id=device(twin(at)), device_id_type=MESH).wait_recv()


def adapt_kernel(count_ref, snap_ref, chosen_ref, steer_ref, all_ref, packed, weights, diag, cov, rhs, inv, go, *scratch):
    at = place()
    greet(at)
    reduce_phase(at, snap_ref, chosen_ref, packed, go, *scratch[:-5])
    solve_phase(count_ref, packed, steer_ref, weights, diag, cov, rhs, inv)
    gather_phase(at, weights, all_ref, *scratch[-5:])


def adapt(snapshots, chosen, train_count, steering):
    bins, gates, channels = snapshots.shape
    looks = steering.shape[1]
    split = snapshots.reshape(SIDE, SIDE, SIDE, 2, gates, channels)
    f32, bf16, sem = jnp.float32, jnp.bfloat16, pltpu.SemaphoreType.DMA
    boxes = [pltpu.VMEM((3,) + (SIDE,) * n + (PACKED, T), f32) for n in (2, 2, 2, 1, 1, 1, 0, 0, 0)]
    vmem = pl.BlockSpec(memory_space=pltpu.VMEM)
    whole = pl.pallas_call(
        adapt_kernel,
        out_shape=jax.ShapeDtypeStruct((SIDE, SIDE, SIDE, 2, channels, looks), bf16),
        in_specs=[pl.BlockSpec(memory_space=pltpu.SMEM), pl.BlockSpec(memory_space=pl.ANY), vmem, vmem],
        out_specs=pl.BlockSpec(memory_space=pl.ANY),
        scratch_shapes=[
            pltpu.VMEM((3, PACKED, T), f32), pltpu.VMEM((channels, looks), bf16), pltpu.VMEM((channels // T, T, T), f32),
            pltpu.VMEM((channels, channels), f32), pltpu.VMEM((channels, looks), f32), pltpu.VMEM((channels // T, T, T), f32),
            pltpu.SemaphoreType.REGULAR,
            pltpu.VMEM((SIDE, SIDE, SIDE, gates, channels), bf16), pltpu.VMEM((SIDE, SIDE, SIDE, gates, channels), bf16),
            pltpu.VMEM((SIDE, SIDE, SIDE, 8, T), f32), pltpu.VMEM((3, SIDE, SIDE, SIDE, PACKED, T), f32), *boxes,
            sem((SIDE,)), sem((SIDE,)), sem((SIDE,)), sem((3, 3)), sem((3, 3)),
            sem((3, 6, SIDE)), sem((3, 6, SIDE)), sem((3, 2, 6)), sem((3, 2, 6)),
            sem, sem((3, 3, 6)), sem((3, 3, 6)), sem((3, 4, 6)), sem((3, 4, 6)),
        ],
        compiler_params=pltpu.CompilerParams(collective_id=1, has_side_effects=True, vmem_limit_bytes=67000000),
        name="adapt",
    )(train_count, split, chosen, steering)
    return whole.reshape(bins, channels, looks)


def apply_kernel(snap_ref, weight_ref, out_ref):
    for b in range(snap_ref.shape[0]):
        out_ref[b] = jnp.dot(snap_ref[b], weight_ref[b], preferred_element_type=jnp.float32).astype(out_ref.dtype)

def beams(snapshots, weights, step=16):
    bins, gates, channels = snapshots.shape
    looks = weights.shape[2]
    return pl.pallas_call(
        apply_kernel,
        grid=(bins // step,),
        out_shape=jax.ShapeDtypeStruct((bins, gates, looks), jnp.bfloat16),
        in_specs=[pl.BlockSpec((step, gates, channels), lambda i: (i, 0, 0)), pl.BlockSpec((step, channels, looks), lambda i: (i, 0, 0))],
        out_specs=pl.BlockSpec((step, gates, looks), lambda i: (i, 0, 0)),
        name="beams",
    )(snapshots, weights)


def body(snapshots, steering, train_list, train_count):
    chosen = selection(train_list, train_count).astype(jnp.float32)
    weights = adapt(snapshots, jnp.broadcast_to(chosen, (8, BLOCK)), train_count, steering[0])
    return beams(snapshots, weights)


def solution(mesh):
    placed = (
        P(None, ("range", "doppler"), None),
        P(("range", "doppler"), None, None),
        P(("range", "doppler"), None),
        P(("range", "doppler")),
    )
    return jax.shard_map(
        body,
        mesh=mesh,
        in_specs=placed,
        out_specs=P(None, ("range", "doppler"), None),
        check_vma=False,
    )
```

```python
import jax
import jax.numpy as jnp
from jax import lax
from jax.experimental import pallas as pl
from jax.experimental.pallas import tpu as pltpu
from jax.sharding import PartitionSpec as P

BLOCK = 128
LOADING = 0.1


def selection(train_list, train_count):
    block_total = train_list.shape[1]
    position = lax.broadcasted_iota(jnp.int32, (1, block_total, 1), 1)
    block_ids = lax.broadcasted_iota(jnp.int32, (1, 1, block_total), 2)
    matches = (train_list[:, :, None] == block_ids) & (position < train_count[:, None, None])
    return jnp.sum(matches.astype(jnp.int32), axis=1)


HI = lax.Precision.HIGHEST
T = BLOCK
def mm(a, b, ca, cb):
    return lax.dot_general(a, b, (((ca,), (cb,)), ((), ())), precision=HI, preferred_element_type=jnp.float32)

def factor_inverse(block):
    lane = lax.broadcasted_iota(jnp.int32, (8, T), 1)
    sub = lax.broadcasted_iota(jnp.int32, (8, T), 0)
    groups = T // 8
    rows = [block[8 * g:8 * g + 8, :] for g in range(groups)]

    def spread(g, k):
        return jnp.broadcast_to(rows[g][:, k:k + 1], (8, T))
    left = [spread(g, 0) for g in range(groups)]
    right = [spread(g, 1) for g in range(groups)]
    for k in range(0, T, 2):
        own, off = k // 8, k % 8
        if k:
            left = [None if f is None else x - f * tips[0] - h * tips[1] for x, f, h in zip(next_left, first, second)]
            right = [None if f is None else x - f * tips[2] - h * tips[3] for x, f, h in zip(next_right, first, second)]
        a, b, d = left[own][off:off + 1], left[own][off + 1:off + 2], right[own][off + 1:off + 2]
        inv = 1.0 / (a * d - b * b)
        aa, ab, bb = d * inv, b * inv, a * inv
        top, low = rows[own][off:off + 1], rows[own][off + 1:off + 2]
        follow = (k + 2) // 8
        if k + 2 < T:
            next_left = [spread(g, k + 2) if g >= follow else None for g in range(groups)]
            next_right = [spread(g, k + 3) if g >= follow else None for g in range(groups)]
            tips = [jnp.broadcast_to(r[:, n:n + 1], (1, T)) for n in (k + 2, k + 3) for r in (top, low)]
        pair = (lane == k) | (lane == k + 1)
        top = jnp.where(pair[:1], jnp.where(lane[:1] == k, 1.0, 0.0), top)
        low = jnp.where(pair[:1], jnp.where(lane[:1] == k, 0.0, 1.0), low)
        first, second = [None] * groups, [None] * groups
        for g in range(follow, groups):
            f = left[g] * aa - right[g] * ab
            h = right[g] * bb - left[g] * ab
            base = jnp.where(pair, 0.0, rows[g])
            if g == own:
                f = jnp.where(sub > off + 1, f, 0.0)
                h = jnp.where(sub > off + 1, h, 0.0)
                base = jnp.where(sub > off + 1, base, rows[g])
            first[g], second[g] = f, h
            rows[g] = base - f * top - h * low
    full = jnp.concatenate(rows, axis=0)
    i = lax.broadcasted_iota(jnp.int32, (T, T), 0)
    j = lax.broadcasted_iota(jnp.int32, (T, T), 1)
    odd = i % 2 == 1
    pivots = jnp.broadcast_to(jnp.sum(jnp.where(i == j, full, 0.0), axis=1, keepdims=True), (T, T))
    below = jnp.sum(jnp.where(odd & (j == i - 1), full, 0.0), axis=1, keepdims=True)
    unit = jnp.where(j < i - i % 2, full, jnp.where(i == j, 1.0, 0.0))
    ratio = jnp.where(odd, below / pltpu.roll(pivots, 1, axis=0), 0.0)
    return (unit - ratio * pltpu.roll(unit, 1, axis=0)) * lax.rsqrt(pivots - below * ratio)


MESH = pl.DeviceIdType.MESH
SIDE = 4
SLICES = 1
ORDERS = (("x", "y", "z"), ("y", "z", "x"), ("z", "x", "y"))

def place():
    r, d = lax.axis_index("range"), lax.axis_index("doppler")
    return {"z": r // SIDE, "y": r % SIDE, "x": d // 2, "c": d % 2}

def device(at):
    return (at["z"] * SIDE + at["y"], at["x"] * 2 + at["c"])

def moved(at, axis, step):
    return {**at, axis: (at[axis] + step) % SIDE}

def twin(at):
    return {**at, "c": 1 - at["c"]}

def greet(at):
    barrier = pltpu.get_barrier_semaphore()
    friends = [moved(at, a, s) for a in "xyz" for s in range(1, SIDE)] + [twin(at)]
    for friend in friends:
        pl.semaphore_signal(barrier, inc=1, device_id=device(friend), device_id_type=MESH)
    pl.semaphore_wait(barrier, len(friends))

HALF = 64
PACKED = 200
CUT = 104
TOP, LOW, ALL = (0, CUT), (CUT, PACKED - CUT), (0, PACKED)
REDUCE = (("z", "y", "x"), ("x", "z", "y"), ("y", "x", "z"))

def cross(a, b):
    return lax.dot_general(a, b, (((0,), (0,)), ((), ())), preferred_element_type=jnp.float32)

def packed_part(part, snaps):
    first, second, third = snaps[:, :T], snaps[:, T:2 * T], snaps[:, 2 * T:]
    i = lax.broadcasted_iota(jnp.int32, (HALF, T), 0)
    j = lax.broadcasted_iota(jnp.int32, (HALF, T), 1)
    if part == 2:
        both = cross(third, jnp.concatenate([first, third], axis=1))
        tile, square = both[:, :T], both[:, T:]
        turned = pltpu.roll(square[:HALF], HALF, axis=1)
        fold = jnp.where(j - HALF > i, turned, square[HALF:])
        ridge = jnp.where(j - HALF == i, turned, 0.0)
    else:
        lo = part * HALF
        lower = cross(first, first)[lo:lo + HALF]
        if part == 0:
            both = cross(second, snaps[:, :2 * T])
            tile, upper = both[:, :T], both[lo:lo + HALF, T:]
        else:
            both = cross(second, snaps[:, T:])
            tile, upper = both[:, T:], both[lo:lo + HALF, :T]
        fold = jnp.where(j <= i + lo, lower, upper)
        ridge = jnp.where(j == i + lo, upper, 0.0)
    return tile, fold, jnp.broadcast_to(jnp.sum(ridge, axis=0, keepdims=True), (8, T))

def unpack(packed, roll):
    i = lax.broadcasted_iota(jnp.int32, (T, T), 0)
    j = lax.broadcasted_iota(jnp.int32, (T, T), 1)
    fold = jnp.concatenate([packed[0, T:T + HALF], packed[1, T:T + HALF]], axis=0)
    ridge = packed[0, PACKED - 8:PACKED - 7] + packed[1, PACKED - 8:PACKED - 7]
    t00 = jnp.where(j <= i, fold, fold.T)
    t11 = jnp.where(j > i, fold, jnp.where(i == j, ridge, fold.T))
    low = packed[2, T:T + HALF]
    mixed = jnp.concatenate([roll(low, HALF, 1), low], axis=0)
    ridge = roll(packed[2, PACKED - 8:], HALF, 1)[:1]
    keep = ((i < HALF) & (j < HALF) & (j > i)) | ((i >= HALF) & (j <= i))
    t22 = jnp.where((i == j) & (i < HALF), ridge, jnp.where(keep, mixed, mixed.T))
    return t00, packed[0, :T], t11, packed[2, :T], packed[1, :T].T, t22

def reduce_phase(at, snap_ref, chosen_ref, out_ref, go, own, other, marks, grams, far1, down1, up1, far2, down2, up2, far3, down3, up3,
                  own_sem, twin_send, twin_recv, mark_send, mark_recv, send1, recv1, send2, recv2):
    twin_at = twin(at)
    me = ((at["z"] * SIDE + at["y"]) * SIDE + at["x"]) * 2
    far = (far1, far2, far3)
    down_in = (down1, down2, down3)
    up_in = (up1, up2, up3)

    def turn(axis, step):
        return (at[axis] + step) % SIDE

    def own_copy(z):
        return pltpu.make_async_copy(snap_ref.at[z, :, :, at["c"]], own.at[z], own_sem.at[z])
    def twin_copy(z):
        return pltpu.make_async_remote_copy(
            src_ref=snap_ref.at[z, :, :, twin_at["c"]], dst_ref=other.at[z], send_sem=twin_send.at[z], recv_sem=twin_recv.at[z],
            device_id=device(twin_at), device_id_type=MESH)
    order = [turn("z", s) for s in (2, 1, 3, 0)]

    def mark_copy(stage, kind):
        ref = marks.at[(at["z"], at["y"], at["x"])[:SIDE - 1 - stage]]
        target = moved(at, "xyz"[stage], kind + 1)
        return pltpu.make_async_remote_copy(
            src_ref=ref, dst_ref=ref, send_sem=mark_send.at[stage, kind], recv_sem=mark_recv.at[stage, kind],
            device_id=device(target), device_id_type=MESH)
    for z in order:
        twin_copy(z).start()
        own_copy(z).start()
    marks[at["z"], at["y"], at["x"]] = jnp.broadcast_to(chosen_ref[...], (8, T))
    for stage in range(3):
        for kind in range(3):
            mark_copy(stage, kind).start()
        for kind in range(3):
            mark_copy(stage, kind).wait_recv()
    for stage in range(3):
        for kind in range(3):
            mark_copy(stage, kind).wait_send()

    lane = lax.broadcasted_iota(jnp.int32, (1, T), 1)
    def ready(z):
        own_copy(z).wait()
        twin_copy(z).wait_recv()
        def mask(n, carry):
            y, x = n // SIDE, n % SIDE
            row = marks[z, y, x][:1]
            for ref, block in ((own, me + at["c"]), (other, me + twin_at["c"])):
                keep = jnp.sum(jnp.where(lane == block, row, 0.0), axis=1, keepdims=True)
                keep = jnp.broadcast_to(keep, (1, ref.shape[-1])).astype(jnp.bfloat16)
                ref[z, y, x] = ref[z, y, x] * keep
            return carry
        lax.fori_loop(0, SIDE * SIDE, mask, 0, unroll=4)

    def compute(part, i3, i2):
        names = REDUCE[part]
        def one(i1, carry):
            where = dict(zip(names, (i3, i2, i1)))
            spot = (where["z"], where["y"], where["x"])
            snaps = jnp.concatenate([own[spot], other[spot]], axis=0)
            tile, fold, ridge = packed_part(part, snaps)
            grams[part, i3, i2, i1, 0:T] = tile
            grams[part, i3, i2, i1, T:T + HALF] = fold
            grams[part, i3, i2, i1, T + HALF:PACKED] = ridge
            return carry
        lax.fori_loop(0, SIDE, one, 0, unroll=True)

    KIND = (
        (2, TOP, "far", 1), (2, LOW, "far", SIDE - 1), (1, LOW, "near", 1),
        (SIDE - 1, TOP, "near", SIDE - 1), (1, TOP, "near", 1), (SIDE - 1, LOW, "near", SIDE - 1),
    )
    def hop(part, stage, kind, chunk=None):
        step, (lo, count), slot, way = KIND[kind]
        names = REDUCE[part]
        prefix = tuple(at[a] for a in names[:stage])
        tail = () if chunk is None else (chunk,)
        rows = (slice(None),) * (2 - stage - len(tail)) + (pl.ds(lo, count), slice(None))
        src = grams.at[(part,) + prefix + (turn(names[stage], step),) + tail + rows]
        box = far[stage] if slot == "far" else (down_in[stage] if way == 1 else up_in[stage])
        dst = box.at[(part,) + tail + rows]
        if chunk is None:
            ss, rs = send2.at[part, stage - 1, kind], recv2.at[part, stage - 1, kind]
        else:
            ss, rs = send1.at[part, kind, chunk], recv1.at[part, kind, chunk]
        return pltpu.make_async_remote_copy(
            src_ref=src, dst_ref=dst, send_sem=ss, recv_sem=rs,
            device_id=device(moved(at, names[stage], way)), device_id_type=MESH)

    def add_far(part, stage, kind, chunk=None):
        names = REDUCE[part]
        prefix = tuple(at[a] for a in names[:stage])
        tail = () if chunk is None else (chunk,)
        step, (lo, count) = (1, TOP) if kind == 0 else (SIDE - 1, LOW)
        whole = (slice(None),) * (2 - stage - len(tail)) + (slice(lo, lo + count), slice(None))
        spot = (part,) + prefix + (turn(names[stage], step),) + tail + whole
        grams[spot] = grams[spot] + far[stage][(part,) + tail + whole]

    def add_near(part, stage, chunk=None):
        names = REDUCE[part]
        tail = () if chunk is None else (chunk,)
        spot = (part,) + tuple(at[a] for a in names[:stage + 1]) + tail
        got = (part,) + tail
        grams[spot] = grams[spot] + down_in[stage][got] + up_in[stage][got]

    def second(part, q):
        return (at[REDUCE[part][1]] + 6 - q) % SIDE

    def loop(body):
        def run(q, carry):
            body(q)
            return carry
        lax.fori_loop(0, SIDE, run, 0)

    leads = at["c"] == 0

    def compute_first(part, i3, i2):
        pl.when(leads)(lambda: compute(part, i3, i2))

    def far_out(part):
        def body(q):
            compute_first(part, turn(REDUCE[part][0], 2), second(part, q))
            hop(part, 0, 0, second(part, q)).start()
            hop(part, 0, 1, second(part, q)).start()
        loop(body)

    ready(order[0])
    pl.when(leads)(lambda: far_out(0))
    for z in order[1:]:
        ready(z)

    @pl.when(jnp.logical_not(leads))
    def _():
        for part in range(3):
            def every(n, carry):
                compute(part, n // SIDE, n % SIDE)
                return carry
            lax.fori_loop(0, SIDE * SIDE, every, 0)
        pl.semaphore_wait(go, 1)
        far_out(0)

    far_out(1)
    far_out(2)

    def near_out(q):
        for part in range(3):
            for step, kind in ((1, 2), (SIDE - 1, 3)):
                compute_first(part, turn(REDUCE[part][0], step), second(part, q))
                hop(part, 0, kind, second(part, q)).start()
    loop(near_out)

    def relay(q):
        for part in range(3):
            compute_first(part, at[REDUCE[part][0]], second(part, q))
        for part in range(3):
            chunk = second(part, q)
            for kind in (0, 1):
                hop(part, 0, kind, chunk).wait_recv()
                add_far(part, 0, kind, chunk)
                hop(part, 0, kind + 4, chunk).start()
    loop(relay)

    for q in range(SIDE):
        for part in range(3):
            chunk = second(part, q)
            for kind in (2, 3, 4, 5):
                hop(part, 0, kind, chunk).wait_recv()
            add_near(part, 0, chunk)
            for kind in ((0, 1), (2,), (), (3,))[q]:
                hop(part, 1, kind).start()
    @pl.when(leads)
    def _():
        pl.semaphore_signal(go, inc=1, device_id=device(twin_at), device_id_type=MESH)

    for stage in (1, 2):
        for part in range(3):
            for kind in (0, 1):
                hop(part, stage, kind).wait_recv()
                add_far(part, stage, kind)
                hop(part, stage, kind + 4).start()
        for part in range(3):
            for kind in (2, 3, 4, 5):
                hop(part, stage, kind).wait_recv()
            add_near(part, stage)
            if stage == 1:
                for kind in range(4):
                    hop(part, 2, kind).start()
    for part in range(3):
        out_ref[part] = grams[(part,) + tuple(at[a] for a in REDUCE[part])]

    for z in order:
        twin_copy(z).wait_send()
    def drain(q):
        for part in range(3):
            for kind in range(6):
                hop(part, 0, kind, q).wait_send()
    loop(drain)
    for part in range(3):
        for stage in (1, 2):
            for kind in range(6):
                hop(part, stage, kind).wait_send()


def solve_phase(count_ref, packed, steer_ref, out_ref, diag, cov, rhs, inv):
    n = cov.shape[0] // T
    scale = (BLOCK * count_ref[0]).astype(jnp.float32)
    i = lax.broadcasted_iota(jnp.int32, (T, T), 0)
    j = lax.broadcasted_iota(jnp.int32, (T, T), 1)
    tiles = unpack(packed, pltpu.roll)
    for (r, c), tile in zip(((0, 0), (1, 0), (1, 1), (2, 0), (2, 1), (2, 2)), tiles):
        tile = tile / scale
        if r == c:
            diag[r] = tile + jnp.where(i == j, LOADING, 0.0)
        else:
            cov[r * T:(r + 1) * T, c * T:(c + 1) * T] = tile
    rhs[...] = steer_ref[...].astype(jnp.float32)

    def forward(b, carry):
        inv[b] = factor_inverse(diag[b])
        for which in range(n):
            def update(b=which):
                lo, hi = b * T, (b + 1) * T
                li = inv[b]
                y = mm(li, rhs[lo:hi, :], 1, 0)
                rhs[lo:hi, :] = y
                if b + 1 < n:
                    panel = mm(cov[hi:, lo:hi], li, 1, 1)
                    cov[hi:, lo:hi] = panel
                    diag[b + 1] = diag[b + 1] - mm(panel[:T], panel[:T], 1, 1)
                    rhs[hi:, :] = rhs[hi:, :] - mm(panel, y, 1, 0)
                if b + 2 < n:
                    diag[b + 2] = diag[b + 2] - mm(panel[T:], panel[T:], 1, 1)
                    cov[hi + T:, hi:hi + T] = cov[hi + T:, hi:hi + T] - mm(panel[T:], panel[:T], 1, 1)
            pl.when(b == which)(update)
        return carry
    lax.fori_loop(0, n, forward, 0)
    for b in reversed(range(n)):
        lo, hi = b * T, (b + 1) * T
        y = rhs[lo:hi, :]
        if b + 1 < n:
            y = y - mm(cov[hi:, lo:hi], rhs[hi:, :], 0, 0)
        rhs[lo:hi, :] = mm(inv[b], y, 0, 0)
    solved = rhs[...]
    response = jnp.sum(steer_ref[...].astype(jnp.float32) * solved, axis=0, keepdims=True)
    out_ref[...] = (solved / response).astype(out_ref.dtype)


def gather_phase(at, own_ref, all_ref, local_sem, send_sem, recv_sem, twin_send, twin_recv):
    rows = own_ref.shape[0] // (3 * SLICES)
    half = rows // 2

    def window(part, gathered, where, halves):
        lo, count = (part * rows, rows) if halves is None else (part * rows + halves * half, half)
        pick = tuple(slice(None) if a in gathered else where[a] for a in "zyx")
        return all_ref.at[pick + (where["c"], pl.ds(lo, count), slice(None))]

    def copy(part, stage, kind, gathered, where, halves, target, send, recv, src=None):
        ref = window(part, gathered, where, halves)
        return pltpu.make_async_remote_copy(
            src_ref=ref if src is None else src, dst_ref=ref, send_sem=send.at[part, stage, kind], recv_sem=recv.at[part, stage, kind],
            device_id=device(target), device_id_type=MESH)

    pending, shared = [], []
    def send(part, stage, kind, gathered, where, halves, target):
        src = own_ref.at[pl.ds(part * rows + halves * half, half)] if stage == 0 and kind < 4 else None
        one = copy(part, stage, kind, gathered, where, halves, target, send_sem, recv_sem, src)
        one.start()
        pending.append(one)
    def arrive(part, stage, kind, gathered, where, halves):
        copy(part, stage, kind, gathered, where, halves, twin(at), send_sem, recv_sem).wait_recv()
    def share(part, stage, kind, gathered, where, halves):
        one = copy(part, stage, kind, gathered, where, halves, twin(at), twin_send, twin_recv)
        one.start()
        shared.append((one, part, stage, kind, gathered, where, halves))

    def around(part, stage):
        names = ORDERS[part // SLICES]
        axis, gathered = names[stage], names[:stage]
        return gathered, moved(at, axis, 1), moved(at, axis, SIDE - 1), moved(at, axis, 2)
    def begin(part, stage):
        gathered, up, down, _ = around(part, stage)
        send(part, stage, 0, gathered, at, 0, up)
        send(part, stage, 1, gathered, at, 1, down)
        send(part, stage, 2, gathered, at, 1, up)
        send(part, stage, 3, gathered, at, 0, down)
    def relay(part, stage):
        gathered, up, down, _ = around(part, stage)
        arrive(part, stage, 0, gathered, down, 0)
        send(part, stage, 4, gathered, down, 0, up)
        share(part, stage, 0, gathered, down, 0)
        arrive(part, stage, 1, gathered, up, 1)
        send(part, stage, 5, gathered, up, 1, down)
        share(part, stage, 1, gathered, up, 1)
    def finish(part, stage, kinds):
        gathered, up, down, far = around(part, stage)
        for kind in kinds:
            where, halves = ((down, 1), (up, 0), (far, 0), (far, 1))[kind - 2]
            arrive(part, stage, kind, gathered, where, halves)
            share(part, stage, kind, gathered, where, halves)

    parts = [[axis * SLICES + piece for axis in range(3)] for piece in range(SLICES)]
    local = pltpu.make_async_copy(own_ref, all_ref.at[at["z"], at["y"], at["x"], at["c"]], local_sem)
    local.start()
    for group in parts:
        for part in group:
            begin(part, 0)
    local.wait()
    for part in range(3 * SLICES):
        share(part, 3, 0, (), at, None)
    for stage in range(3):
        for group in parts:
            for part in group:
                relay(part, stage)
            for part in group:
                finish(part, stage, (2, 3))
            for part in group:
                finish(part, stage, (4, 5))
                if stage < 2:
                    begin(part, stage + 1)
    for one in pending:
        one.wait_send()
    for one, part, stage, kind, gathered, where, halves in shared:
        one.wait_send()
        copy(part, stage, kind, gathered, twin(where), halves, twin(at), twin_send, twin_recv).wait_recv()


def adapt_kernel(count_ref, snap_ref, chosen_ref, steer_ref, all_ref, packed, weights, diag, cov, rhs, inv, go, *scratch):
    at = place()
    greet(at)
    reduce_phase(at, snap_ref, chosen_ref, packed, go, *scratch[:-5])
    solve_phase(count_ref, packed, steer_ref, weights, diag, cov, rhs, inv)
    gather_phase(at, weights, all_ref, *scratch[-5:])


def adapt(snapshots, chosen, train_count, steering):
    bins, gates, channels = snapshots.shape
    looks = steering.shape[1]
    split = snapshots.reshape(SIDE, SIDE, SIDE, 2, gates, channels)
    f32, bf16, sem = jnp.float32, jnp.bfloat16, pltpu.SemaphoreType.DMA
    boxes = [pltpu.VMEM((3,) + (SIDE,) * n + (PACKED, T), f32) for n in (2, 2, 2, 1, 1, 1, 0, 0, 0)]
    vmem = pl.BlockSpec(memory_space=pltpu.VMEM)
    whole = pl.pallas_call(
        adapt_kernel,
        out_shape=jax.ShapeDtypeStruct((SIDE, SIDE, SIDE, 2, channels, looks), bf16),
        in_specs=[pl.BlockSpec(memory_space=pltpu.SMEM), pl.BlockSpec(memory_space=pl.ANY), vmem, vmem],
        out_specs=pl.BlockSpec(memory_space=pl.ANY),
        scratch_shapes=[
            pltpu.VMEM((3, PACKED, T), f32), pltpu.VMEM((channels, looks), bf16), pltpu.VMEM((channels // T, T, T), f32),
            pltpu.VMEM((channels, channels), f32), pltpu.VMEM((channels, looks), f32), pltpu.VMEM((channels // T, T, T), f32),
            pltpu.SemaphoreType.REGULAR,
            pltpu.VMEM((SIDE, SIDE, SIDE, gates, channels), bf16), pltpu.VMEM((SIDE, SIDE, SIDE, gates, channels), bf16),
            pltpu.VMEM((SIDE, SIDE, SIDE, 8, T), f32), pltpu.VMEM((3, SIDE, SIDE, SIDE, PACKED, T), f32), *boxes,
            sem((SIDE,)), sem((SIDE,)), sem((SIDE,)), sem((3, 3)), sem((3, 3)),
            sem((3, 6, SIDE)), sem((3, 6, SIDE)), sem((3, 2, 6)), sem((3, 2, 6)),
            sem, *[sem((3 * SLICES, n, 6)) for n in (3, 3, 4, 4)],
        ],
        compiler_params=pltpu.CompilerParams(collective_id=1, has_side_effects=True, vmem_limit_bytes=67000000),
        name="adapt",
    )(train_count, split, chosen, steering)
    return whole.reshape(bins, channels, looks)


def apply_kernel(snap_ref, weight_ref, out_ref):
    for b in range(snap_ref.shape[0]):
        out_ref[b] = jnp.dot(snap_ref[b], weight_ref[b], preferred_element_type=jnp.float32).astype(out_ref.dtype)

def beams(snapshots, weights, step=32):
    bins, gates, channels = snapshots.shape
    looks = weights.shape[2]
    return pl.pallas_call(
        apply_kernel,
        grid=(bins // step,),
        out_shape=jax.ShapeDtypeStruct((bins, gates, looks), jnp.bfloat16),
        in_specs=[pl.BlockSpec((step, gates, channels), lambda i: (i, 0, 0)), pl.BlockSpec((step, channels, looks), lambda i: (i, 0, 0))],
        out_specs=pl.BlockSpec((step, gates, looks), lambda i: (i, 0, 0)),
        name="beams",
    )(snapshots, weights)


def body(snapshots, steering, train_list, train_count):
    chosen = selection(train_list, train_count).astype(jnp.float32)
    weights = adapt(snapshots, chosen, train_count, steering[0])
    return beams(snapshots, weights)


def solution(mesh):
    placed = (
        P(None, ("range", "doppler"), None),
        P(("range", "doppler"), None, None),
        P(("range", "doppler"), None),
        P(("range", "doppler")),
    )
    return jax.shard_map(
        body,
        mesh=mesh,
        in_specs=placed,
        out_specs=P(None, ("range", "doppler"), None),
        check_vma=False,
    )
```

```python
import jax
import jax.numpy as jnp
from jax import lax
from jax.experimental import pallas as pl
from jax.experimental.pallas import tpu as pltpu
from jax.sharding import PartitionSpec as P

BLOCK = 128
LOADING = 0.1


def selection(train_list, train_count):
    block_total = train_list.shape[1]
    position = lax.broadcasted_iota(jnp.int32, (1, block_total, 1), 1)
    block_ids = lax.broadcasted_iota(jnp.int32, (1, 1, block_total), 2)
    matches = (train_list[:, :, None] == block_ids) & (position < train_count[:, None, None])
    return jnp.sum(matches.astype(jnp.int32), axis=1)


HI = lax.Precision.HIGHEST
T = BLOCK
def mm(a, b, ca, cb):
    return lax.dot_general(a, b, (((ca,), (cb,)), ((), ())), precision=HI, preferred_element_type=jnp.float32)

def factor_inverse(block):
    lane = lax.broadcasted_iota(jnp.int32, (8, T), 1)
    sub = lax.broadcasted_iota(jnp.int32, (8, T), 0)
    groups = T // 8
    rows = [block[8 * g:8 * g + 8, :] for g in range(groups)]

    def spread(g, k):
        return jnp.broadcast_to(rows[g][:, k:k + 1], (8, T))
    left = [spread(g, 0) for g in range(groups)]
    right = [spread(g, 1) for g in range(groups)]
    for k in range(0, T, 2):
        own, off = k // 8, k % 8
        if k:
            left = [None if f is None else x - f * tips[0] - h * tips[1] for x, f, h in zip(next_left, first, second)]
            right = [None if f is None else x - f * tips[2] - h * tips[3] for x, f, h in zip(next_right, first, second)]
        a, b, d = left[own][off:off + 1], left[own][off + 1:off + 2], right[own][off + 1:off + 2]
        inv = 1.0 / (a * d - b * b)
        aa, ab, bb = d * inv, b * inv, a * inv
        top, low = rows[own][off:off + 1], rows[own][off + 1:off + 2]
        follow = (k + 2) // 8
        if k + 2 < T:
            next_left = [spread(g, k + 2) if g >= follow else None for g in range(groups)]
            next_right = [spread(g, k + 3) if g >= follow else None for g in range(groups)]
            tips = [jnp.broadcast_to(r[:, n:n + 1], (1, T)) for n in (k + 2, k + 3) for r in (top, low)]
        pair = (lane == k) | (lane == k + 1)
        top = jnp.where(pair[:1], jnp.where(lane[:1] == k, 1.0, 0.0), top)
        low = jnp.where(pair[:1], jnp.where(lane[:1] == k, 0.0, 1.0), low)
        first, second = [None] * groups, [None] * groups
        for g in range(follow, groups):
            f = left[g] * aa - right[g] * ab
            h = right[g] * bb - left[g] * ab
            base = jnp.where(pair, 0.0, rows[g])
            if g == own:
                f = jnp.where(sub > off + 1, f, 0.0)
                h = jnp.where(sub > off + 1, h, 0.0)
                base = jnp.where(sub > off + 1, base, rows[g])
            first[g], second[g] = f, h
            rows[g] = base - f * top - h * low
    full = jnp.concatenate(rows, axis=0)
    i = lax.broadcasted_iota(jnp.int32, (T, T), 0)
    j = lax.broadcasted_iota(jnp.int32, (T, T), 1)
    odd = i % 2 == 1
    pivots = jnp.broadcast_to(jnp.sum(jnp.where(i == j, full, 0.0), axis=1, keepdims=True), (T, T))
    below = jnp.sum(jnp.where(odd & (j == i - 1), full, 0.0), axis=1, keepdims=True)
    unit = jnp.where(j < i - i % 2, full, jnp.where(i == j, 1.0, 0.0))
    ratio = jnp.where(odd, below / pltpu.roll(pivots, 1, axis=0), 0.0)
    return (unit - ratio * pltpu.roll(unit, 1, axis=0)) * lax.rsqrt(pivots - below * ratio)


MESH = pl.DeviceIdType.MESH
SIDE = 4
SLICES = 1
ORDERS = (("x", "y", "z"), ("y", "z", "x"), ("z", "x", "y"))

def place():
    r, d = lax.axis_index("range"), lax.axis_index("doppler")
    return {"z": r // SIDE, "y": r % SIDE, "x": d // 2, "c": d % 2}

def device(at):
    return (at["z"] * SIDE + at["y"], at["x"] * 2 + at["c"])

def moved(at, axis, step):
    return {**at, axis: (at[axis] + step) % SIDE}

def twin(at):
    return {**at, "c": 1 - at["c"]}

def greet(at):
    barrier = pltpu.get_barrier_semaphore()
    friends = [moved(at, a, s) for a in "xyz" for s in range(1, SIDE)] + [twin(at)]
    for friend in friends:
        pl.semaphore_signal(barrier, inc=1, device_id=device(friend), device_id_type=MESH)
    pl.semaphore_wait(barrier, len(friends))

HALF = 64
PACKED = 200
CUT = 104
TOP, LOW, ALL = (0, CUT), (CUT, PACKED - CUT), (0, PACKED)
REDUCE = (("z", "y", "x"), ("x", "z", "y"), ("y", "x", "z"))

def cross(a, b):
    return lax.dot_general(a, b, (((0,), (0,)), ((), ())), preferred_element_type=jnp.float32)

def packed_part(part, snaps):
    first, second, third = snaps[:, :T], snaps[:, T:2 * T], snaps[:, 2 * T:]
    i = lax.broadcasted_iota(jnp.int32, (HALF, T), 0)
    j = lax.broadcasted_iota(jnp.int32, (HALF, T), 1)
    if part == 2:
        both = cross(third, jnp.concatenate([first, third], axis=1))
        tile, square = both[:, :T], both[:, T:]
        turned = pltpu.roll(square[:HALF], HALF, axis=1)
        fold = jnp.where(j - HALF > i, turned, square[HALF:])
        ridge = jnp.where(j - HALF == i, turned, 0.0)
    else:
        lo = part * HALF
        lower = cross(first, first)[lo:lo + HALF]
        if part == 0:
            both = cross(second, snaps[:, :2 * T])
            tile, upper = both[:, :T], both[lo:lo + HALF, T:]
        else:
            both = cross(second, snaps[:, T:])
            tile, upper = both[:, T:], both[lo:lo + HALF, :T]
        fold = jnp.where(j <= i + lo, lower, upper)
        ridge = jnp.where(j == i + lo, upper, 0.0)
    return tile, fold, jnp.broadcast_to(jnp.sum(ridge, axis=0, keepdims=True), (8, T))

def unpack(packed, roll):
    i = lax.broadcasted_iota(jnp.int32, (T, T), 0)
    j = lax.broadcasted_iota(jnp.int32, (T, T), 1)
    fold = jnp.concatenate([packed[0, T:T + HALF], packed[1, T:T + HALF]], axis=0)
    ridge = packed[0, PACKED - 8:PACKED - 7] + packed[1, PACKED - 8:PACKED - 7]
    t00 = jnp.where(j <= i, fold, fold.T)
    t11 = jnp.where(j > i, fold, jnp.where(i == j, ridge, fold.T))
    low = packed[2, T:T + HALF]
    mixed = jnp.concatenate([roll(low, HALF, 1), low], axis=0)
    ridge = roll(packed[2, PACKED - 8:], HALF, 1)[:1]
    keep = ((i < HALF) & (j < HALF) & (j > i)) | ((i >= HALF) & (j <= i))
    t22 = jnp.where((i == j) & (i < HALF), ridge, jnp.where(keep, mixed, mixed.T))
    return t00, packed[0, :T], t11, packed[2, :T], packed[1, :T].T, t22

def reduce_phase(at, snap_ref, chosen_ref, out_ref, go, own, other, marks, grams, far1, down1, up1, far2, down2, up2, far3, down3, up3,
                  own_sem, twin_send, twin_recv, mark_send, mark_recv, send1, recv1, send2, recv2):
    twin_at = twin(at)
    me = ((at["z"] * SIDE + at["y"]) * SIDE + at["x"]) * 2
    far = (far1, far2, far3)
    down_in = (down1, down2, down3)
    up_in = (up1, up2, up3)

    def turn(axis, step):
        return (at[axis] + step) % SIDE

    def own_copy(z):
        return pltpu.make_async_copy(snap_ref.at[z, :, :, at["c"]], own.at[z], own_sem.at[z])
    def twin_copy(z):
        return pltpu.make_async_remote_copy(
            src_ref=snap_ref.at[z, :, :, twin_at["c"]], dst_ref=other.at[z], send_sem=twin_send.at[z], recv_sem=twin_recv.at[z],
            device_id=device(twin_at), device_id_type=MESH)
    order = [turn("z", s) for s in (2, 1, 3, 0)]

    def mark_copy(stage, kind):
        ref = marks.at[(at["z"], at["y"], at["x"])[:SIDE - 1 - stage]]
        target = moved(at, "xyz"[stage], kind + 1)
        return pltpu.make_async_remote_copy(
            src_ref=ref, dst_ref=ref, send_sem=mark_send.at[stage, kind], recv_sem=mark_recv.at[stage, kind],
            device_id=device(target), device_id_type=MESH)
    for z in order:
        twin_copy(z).start()
        own_copy(z).start()
    marks[at["z"], at["y"], at["x"]] = jnp.broadcast_to(chosen_ref[...], (8, T))
    for stage in range(3):
        for kind in range(3):
            mark_copy(stage, kind).start()
        for kind in range(3):
            mark_copy(stage, kind).wait_recv()
    for stage in range(3):
        for kind in range(3):
            mark_copy(stage, kind).wait_send()

    lane = lax.broadcasted_iota(jnp.int32, (1, T), 1)
    def ready(z):
        own_copy(z).wait()
        twin_copy(z).wait_recv()
        def mask(n, carry):
            y, x = n // SIDE, n % SIDE
            row = marks[z, y, x][:1]
            for ref, block in ((own, me + at["c"]), (other, me + twin_at["c"])):
                keep = jnp.sum(jnp.where(lane == block, row, 0.0), axis=1, keepdims=True)
                keep = jnp.broadcast_to(keep, (1, ref.shape[-1])).astype(jnp.bfloat16)
                ref[z, y, x] = ref[z, y, x] * keep
            return carry
        lax.fori_loop(0, SIDE * SIDE, mask, 0, unroll=4)

    def compute(part, i3, i2):
        names = REDUCE[part]
        def one(i1, carry):
            where = dict(zip(names, (i3, i2, i1)))
            spot = (where["z"], where["y"], where["x"])
            snaps = jnp.concatenate([own[spot], other[spot]], axis=0)
            tile, fold, ridge = packed_part(part, snaps)
            grams[part, i3, i2, i1, 0:T] = tile
            grams[part, i3, i2, i1, T:T + HALF] = fold
            grams[part, i3, i2, i1, T + HALF:PACKED] = ridge
            return carry
        lax.fori_loop(0, SIDE, one, 0, unroll=True)

    KIND = (
        (2, TOP, "far", 1), (2, LOW, "far", SIDE - 1), (1, LOW, "near", 1),
        (SIDE - 1, TOP, "near", SIDE - 1), (1, TOP, "near", 1), (SIDE - 1, LOW, "near", SIDE - 1),
    )
    def hop(part, stage, kind, chunk=None):
        step, (lo, count), slot, way = KIND[kind]
        names = REDUCE[part]
        prefix = tuple(at[a] for a in names[:stage])
        tail = () if chunk is None else (chunk,)
        rows = (slice(None),) * (2 - stage - len(tail)) + (pl.ds(lo, count), slice(None))
        src = grams.at[(part,) + prefix + (turn(names[stage], step),) + tail + rows]
        box = far[stage] if slot == "far" else (down_in[stage] if way == 1 else up_in[stage])
        dst = box.at[(part,) + tail + rows]
        if chunk is None:
            ss, rs = send2.at[part, stage - 1, kind], recv2.at[part, stage - 1, kind]
        else:
            ss, rs = send1.at[part, kind, chunk], recv1.at[part, kind, chunk]
        return pltpu.make_async_remote_copy(
            src_ref=src, dst_ref=dst, send_sem=ss, recv_sem=rs,
            device_id=device(moved(at, names[stage], way)), device_id_type=MESH)

    def add_far(part, stage, kind, chunk=None):
        names = REDUCE[part]
        prefix = tuple(at[a] for a in names[:stage])
        tail = () if chunk is None else (chunk,)
        step, (lo, count) = (1, TOP) if kind == 0 else (SIDE - 1, LOW)
        whole = (slice(None),) * (2 - stage - len(tail)) + (slice(lo, lo + count), slice(None))
        spot = (part,) + prefix + (turn(names[stage], step),) + tail + whole
        grams[spot] = grams[spot] + far[stage][(part,) + tail + whole]

    def add_near(part, stage, chunk=None):
        names = REDUCE[part]
        tail = () if chunk is None else (chunk,)
        spot = (part,) + tuple(at[a] for a in names[:stage + 1]) + tail
        got = (part,) + tail
        grams[spot] = grams[spot] + down_in[stage][got] + up_in[stage][got]

    def second(part, q):
        return (at[REDUCE[part][1]] + 6 - q) % SIDE

    def loop(body):
        def run(q, carry):
            body(q)
            return carry
        lax.fori_loop(0, SIDE, run, 0)

    leads = at["c"] == 0

    def compute_first(part, i3, i2):
        pl.when(leads)(lambda: compute(part, i3, i2))

    def far_out(part):
        def body(q):
            compute_first(part, turn(REDUCE[part][0], 2), second(part, q))
            hop(part, 0, 0, second(part, q)).start()
            hop(part, 0, 1, second(part, q)).start()
        loop(body)

    ready(order[0])
    pl.when(leads)(lambda: far_out(0))
    for z in order[1:]:
        ready(z)

    @pl.when(jnp.logical_not(leads))
    def _():
        for part in range(3):
            def every(n, carry):
                compute(part, n // SIDE, n % SIDE)
                return carry
            lax.fori_loop(0, SIDE * SIDE, every, 0)
        pl.semaphore_wait(go, 1)
        far_out(0)

    far_out(1)
    far_out(2)

    def near_out(q):
        for part in range(3):
            for step, kind in ((1, 2), (SIDE - 1, 3)):
                compute_first(part, turn(REDUCE[part][0], step), second(part, q))
                hop(part, 0, kind, second(part, q)).start()
    loop(near_out)

    def relay(q):
        for part in range(3):
            compute_first(part, at[REDUCE[part][0]], second(part, q))
        for part in range(3):
            chunk = second(part, q)
            for kind in (0, 1):
                hop(part, 0, kind, chunk).wait_recv()
                add_far(part, 0, kind, chunk)
                hop(part, 0, kind + 4, chunk).start()
    loop(relay)

    for q in range(SIDE):
        for part in range(3):
            chunk = second(part, q)
            for kind in (2, 3, 4, 5):
                hop(part, 0, kind, chunk).wait_recv()
            add_near(part, 0, chunk)
            for kind in ((0, 1), (2,), (), (3,))[q]:
                hop(part, 1, kind).start()
    @pl.when(leads)
    def _():
        pl.semaphore_signal(go, inc=1, device_id=device(twin_at), device_id_type=MESH)

    for stage in (1, 2):
        for part in range(3):
            for kind in (0, 1):
                hop(part, stage, kind).wait_recv()
                add_far(part, stage, kind)
                hop(part, stage, kind + 4).start()
        for part in range(3):
            for kind in (2, 3, 4, 5):
                hop(part, stage, kind).wait_recv()
            add_near(part, stage)
            if stage == 1:
                for kind in range(4):
                    hop(part, 2, kind).start()
    for part in range(3):
        out_ref[part] = grams[(part,) + tuple(at[a] for a in REDUCE[part])]

    for z in order:
        twin_copy(z).wait_send()
    def drain(q):
        for part in range(3):
            for kind in range(6):
                hop(part, 0, kind, q).wait_send()
    loop(drain)
    for part in range(3):
        for stage in (1, 2):
            for kind in range(6):
                hop(part, stage, kind).wait_send()


def solve_phase(count_ref, packed, steer_ref, out_ref, diag, cov, rhs, inv):
    n = cov.shape[0] // T
    scale = (BLOCK * count_ref[0]).astype(jnp.float32)
    i = lax.broadcasted_iota(jnp.int32, (T, T), 0)
    j = lax.broadcasted_iota(jnp.int32, (T, T), 1)
    tiles = unpack(packed, pltpu.roll)
    for (r, c), tile in zip(((0, 0), (1, 0), (1, 1), (2, 0), (2, 1), (2, 2)), tiles):
        tile = tile / scale
        if r == c:
            diag[r] = tile + jnp.where(i == j, LOADING, 0.0)
        else:
            cov[r * T:(r + 1) * T, c * T:(c + 1) * T] = tile
    rhs[...] = steer_ref[...].astype(jnp.float32)

    def forward(b, carry):
        inv[b] = factor_inverse(diag[b])
        for which in range(n):
            def update(b=which):
                lo, hi = b * T, (b + 1) * T
                li = inv[b]
                y = mm(li, rhs[lo:hi, :], 1, 0)
                rhs[lo:hi, :] = y
                if b + 1 < n:
                    panel = mm(cov[hi:, lo:hi], li, 1, 1)
                    cov[hi:, lo:hi] = panel
                    diag[b + 1] = diag[b + 1] - mm(panel[:T], panel[:T], 1, 1)
                    rhs[hi:, :] = rhs[hi:, :] - mm(panel, y, 1, 0)
                if b + 2 < n:
                    diag[b + 2] = diag[b + 2] - mm(panel[T:], panel[T:], 1, 1)
                    cov[hi + T:, hi:hi + T] = cov[hi + T:, hi:hi + T] - mm(panel[T:], panel[:T], 1, 1)
            pl.when(b == which)(update)
        return carry
    lax.fori_loop(0, n, forward, 0)
    for b in reversed(range(n)):
        lo, hi = b * T, (b + 1) * T
        y = rhs[lo:hi, :]
        if b + 1 < n:
            y = y - mm(cov[hi:, lo:hi], rhs[hi:, :], 0, 0)
        rhs[lo:hi, :] = mm(inv[b], y, 0, 0)
    solved = rhs[...]
    response = jnp.sum(steer_ref[...].astype(jnp.float32) * solved, axis=0, keepdims=True)
    out_ref[...] = (solved / response).astype(out_ref.dtype)


def gather_phase(at, own_ref, all_ref, local_sem, send_sem, recv_sem, twin_send, twin_recv):
    rows = own_ref.shape[0] // (3 * SLICES)
    half = rows // 2

    def window(part, gathered, where, halves):
        lo, count = (part * rows, rows) if halves is None else (part * rows + halves * half, half)
        pick = tuple(slice(None) if a in gathered else where[a] for a in "zyx")
        return all_ref.at[pick + (where["c"], pl.ds(lo, count), slice(None))]

    def copy(part, stage, kind, gathered, where, halves, target, send, recv, src=None):
        ref = window(part, gathered, where, halves)
        return pltpu.make_async_remote_copy(
            src_ref=ref if src is None else src, dst_ref=ref, send_sem=send.at[part, stage, kind], recv_sem=recv.at[part, stage, kind],
            device_id=device(target), device_id_type=MESH)

    pending, shared = [], []
    def send(part, stage, kind, gathered, where, halves, target):
        src = own_ref.at[pl.ds(part * rows + halves * half, half)] if stage == 0 else None
        one = copy(part, stage, kind, gathered, where, halves, target, send_sem, recv_sem, src)
        one.start()
        pending.append(one)
    def arrive(part, stage, kind, gathered, where, halves):
        copy(part, stage, kind, gathered, where, halves, twin(at), send_sem, recv_sem).wait_recv()
    def share(part, stage, kind, gathered, where, halves):
        one = copy(part, stage, kind, gathered, where, halves, twin(at), twin_send, twin_recv)
        one.start()
        shared.append((one, part, stage, kind, gathered, where, halves))

    def around(part, stage):
        names = ORDERS[part // SLICES]
        axis, gathered = names[stage], names[:stage]
        return gathered, moved(at, axis, 1), moved(at, axis, SIDE - 1), moved(at, axis, 2)
    def begin(part, stage):
        gathered, up, down, far = around(part, stage)
        send(part, stage, 0, gathered, at, 0, up)
        send(part, stage, 1, gathered, at, 1, down)
        send(part, stage, 2, gathered, at, 1, up)
        send(part, stage, 3, gathered, at, 0, down)
        if stage == 0:
            send(part, stage, 4, gathered, at, 0, far)
            send(part, stage, 5, gathered, at, 1, far)
    def relay(part, stage):
        gathered, up, down, _ = around(part, stage)
        arrive(part, stage, 0, gathered, down, 0)
        if stage:
            send(part, stage, 4, gathered, down, 0, up)
        share(part, stage, 0, gathered, down, 0)
        arrive(part, stage, 1, gathered, up, 1)
        if stage:
            send(part, stage, 5, gathered, up, 1, down)
        share(part, stage, 1, gathered, up, 1)
    def finish(part, stage, kinds):
        gathered, up, down, far = around(part, stage)
        for kind in kinds:
            where, halves = ((down, 1), (up, 0), (far, 0), (far, 1))[kind - 2]
            arrive(part, stage, kind, gathered, where, halves)
            share(part, stage, kind, gathered, where, halves)

    parts = [[axis * SLICES + piece for axis in range(3)] for piece in range(SLICES)]
    local = pltpu.make_async_copy(own_ref, all_ref.at[at["z"], at["y"], at["x"], at["c"]], local_sem)
    local.start()
    for group in parts:
        for part in group:
            begin(part, 0)
    local.wait()
    for part in range(3 * SLICES):
        share(part, 3, 0, (), at, None)
    for stage in range(3):
        for group in parts:
            for part in group:
                relay(part, stage)
            for part in group:
                finish(part, stage, (2, 3))
            for part in group:
                finish(part, stage, (4, 5))
                if stage < 2:
                    begin(part, stage + 1)
    for one in pending:
        one.wait_send()
    for one, part, stage, kind, gathered, where, halves in shared:
        one.wait_send()
        copy(part, stage, kind, gathered, twin(where), halves, twin(at), twin_send, twin_recv).wait_recv()


def adapt_kernel(count_ref, snap_ref, chosen_ref, steer_ref, all_ref, packed, weights, diag, cov, rhs, inv, go, *scratch):
    at = place()
    greet(at)
    reduce_phase(at, snap_ref, chosen_ref, packed, go, *scratch[:-5])
    solve_phase(count_ref, packed, steer_ref, weights, diag, cov, rhs, inv)
    gather_phase(at, weights, all_ref, *scratch[-5:])


def adapt(snapshots, chosen, train_count, steering):
    bins, gates, channels = snapshots.shape
    looks = steering.shape[1]
    split = snapshots.reshape(SIDE, SIDE, SIDE, 2, gates, channels)
    f32, bf16, sem = jnp.float32, jnp.bfloat16, pltpu.SemaphoreType.DMA
    boxes = [pltpu.VMEM((3,) + (SIDE,) * n + (PACKED, T), f32) for n in (2, 2, 2, 1, 1, 1, 0, 0, 0)]
    vmem = pl.BlockSpec(memory_space=pltpu.VMEM)
    whole = pl.pallas_call(
        adapt_kernel,
        out_shape=jax.ShapeDtypeStruct((SIDE, SIDE, SIDE, 2, channels, looks), bf16),
        in_specs=[pl.BlockSpec(memory_space=pltpu.SMEM), pl.BlockSpec(memory_space=pl.ANY), vmem, vmem],
        out_specs=pl.BlockSpec(memory_space=pl.ANY),
        scratch_shapes=[
            pltpu.VMEM((3, PACKED, T), f32), pltpu.VMEM((channels, looks), bf16), pltpu.VMEM((channels // T, T, T), f32),
            pltpu.VMEM((channels, channels), f32), pltpu.VMEM((channels, looks), f32), pltpu.VMEM((channels // T, T, T), f32),
            pltpu.SemaphoreType.REGULAR,
            pltpu.VMEM((SIDE, SIDE, SIDE, gates, channels), bf16), pltpu.VMEM((SIDE, SIDE, SIDE, gates, channels), bf16),
            pltpu.VMEM((SIDE, SIDE, SIDE, 8, T), f32), pltpu.VMEM((3, SIDE, SIDE, SIDE, PACKED, T), f32), *boxes,
            sem((SIDE,)), sem((SIDE,)), sem((SIDE,)), sem((3, 3)), sem((3, 3)),
            sem((3, 6, SIDE)), sem((3, 6, SIDE)), sem((3, 2, 6)), sem((3, 2, 6)),
            sem, *[sem((3 * SLICES, n, 6)) for n in (3, 3, 4, 4)],
        ],
        compiler_params=pltpu.CompilerParams(collective_id=1, has_side_effects=True, vmem_limit_bytes=67000000),
        name="adapt",
    )(train_count, split, chosen, steering)
    return whole.reshape(bins, channels, looks)


def apply_kernel(snap_hbm, weight_hbm, out_hbm, snaps, weights, outs, snap_sem, weight_sem, out_sem):
    chunks = snap_sem.shape[0]
    step = snaps.shape[0] // chunks

    def part(n):
        return pl.ds(pl.multiple_of(n * step, step), step)
    def snap_copy(n):
        return pltpu.make_async_copy(snap_hbm.at[part(n)], snaps.at[part(n)], snap_sem.at[n])
    def weight_copy(n):
        return pltpu.make_async_copy(weight_hbm.at[part(n)], weights.at[part(n)], weight_sem.at[n])
    def out_copy(n):
        return pltpu.make_async_copy(outs.at[part(n)], out_hbm.at[part(n)], out_sem.at[n])

    def fetch(n, carry):
        snap_copy(n).start()
        weight_copy(n).start()
        return carry
    lax.fori_loop(0, chunks, fetch, 0)
    def multiply(n, carry):
        snap_copy(n).wait()
        weight_copy(n).wait()
        for b in range(step):
            at = n * step + b
            outs[at] = jnp.dot(snaps[at], weights[at], preferred_element_type=jnp.float32).astype(outs.dtype)
        out_copy(n).start()
        return carry
    lax.fori_loop(0, chunks, multiply, 0)
    def drain(n, carry):
        out_copy(n).wait()
        return carry
    lax.fori_loop(0, chunks, drain, 0)


def beams(snapshots, weights, chunks=16):
    bins, gates, channels = snapshots.shape
    looks = weights.shape[2]
    bf16, sem, whole = jnp.bfloat16, pltpu.SemaphoreType.DMA, pl.BlockSpec(memory_space=pl.ANY)
    return pl.pallas_call(
        apply_kernel,
        out_shape=jax.ShapeDtypeStruct((bins, gates, looks), bf16),
        in_specs=[whole, whole],
        out_specs=whole,
        scratch_shapes=[
            pltpu.VMEM((bins, gates, channels), bf16), pltpu.VMEM((bins, channels, looks), bf16), pltpu.VMEM((bins, gates, looks), bf16),
            sem((chunks,)), sem((chunks,)), sem((chunks,)),
        ],
        compiler_params=pltpu.CompilerParams(vmem_limit_bytes=60 * 1024 * 1024),
        name="beams",
    )(snapshots, weights)


def body(snapshots, steering, train_list, train_count):
    chosen = selection(train_list, train_count).astype(jnp.float32)
    weights = adapt(snapshots, chosen, train_count, steering[0])
    return beams(snapshots, weights)


def solution(mesh):
    placed = (
        P(None, ("range", "doppler"), None),
        P(("range", "doppler"), None, None),
        P(("range", "doppler"), None),
        P(("range", "doppler")),
    )
    return jax.shard_map(
        body,
        mesh=mesh,
        in_specs=placed,
        out_specs=P(None, ("range", "doppler"), None),
        check_vma=False,
    )
```

```python
import jax
import jax.numpy as jnp
from jax import lax
from jax.experimental import pallas as pl
from jax.experimental.pallas import tpu as pltpu
from jax.sharding import PartitionSpec as P

BLOCK = 128
LOADING = 0.1


def selection(order, count):
    block = lax.broadcasted_iota(jnp.int32, (BLOCK, BLOCK), 0)
    position = lax.broadcasted_iota(jnp.int32, (BLOCK, BLOCK), 1)
    matches = jnp.where((order == block) & (position < count), 1.0, 0.0)
    ones = jnp.ones((8, BLOCK), jnp.float32)
    return lax.dot_general(ones, matches, (((1,), (1,)), ((), ())), preferred_element_type=jnp.float32)


HI = lax.Precision.HIGHEST
T = BLOCK
def mm(a, b, ca, cb):
    return lax.dot_general(a, b, (((ca,), (cb,)), ((), ())), precision=HI, preferred_element_type=jnp.float32)

def factor_inverse(block):
    lane = lax.broadcasted_iota(jnp.int32, (8, T), 1)
    sub = lax.broadcasted_iota(jnp.int32, (8, T), 0)
    groups = T // 8
    rows = [block[8 * g:8 * g + 8, :] for g in range(groups)]

    def spread(g, k):
        return jnp.broadcast_to(rows[g][:, k:k + 1], (8, T))
    left = [spread(g, 0) for g in range(groups)]
    right = [spread(g, 1) for g in range(groups)]
    for k in range(0, T, 2):
        own, off = k // 8, k % 8
        if k:
            left = [None if f is None else x - f * tips[0] - h * tips[1] for x, f, h in zip(next_left, first, second)]
            right = [None if f is None else x - f * tips[2] - h * tips[3] for x, f, h in zip(next_right, first, second)]
        a, b, d = left[own][off:off + 1], left[own][off + 1:off + 2], right[own][off + 1:off + 2]
        inv = 1.0 / (a * d - b * b)
        aa, ab, bb = d * inv, b * inv, a * inv
        top, low = rows[own][off:off + 1], rows[own][off + 1:off + 2]
        follow = (k + 2) // 8
        if k + 2 < T:
            next_left = [spread(g, k + 2) if g >= follow else None for g in range(groups)]
            next_right = [spread(g, k + 3) if g >= follow else None for g in range(groups)]
            tips = [jnp.broadcast_to(r[:, n:n + 1], (1, T)) for n in (k + 2, k + 3) for r in (top, low)]
        pair = (lane == k) | (lane == k + 1)
        top = jnp.where(pair[:1], jnp.where(lane[:1] == k, 1.0, 0.0), top)
        low = jnp.where(pair[:1], jnp.where(lane[:1] == k, 0.0, 1.0), low)
        first, second = [None] * groups, [None] * groups
        for g in range(follow, groups):
            f = left[g] * aa - right[g] * ab
            h = right[g] * bb - left[g] * ab
            base = jnp.where(pair, 0.0, rows[g])
            if g == own:
                f = jnp.where(sub > off + 1, f, 0.0)
                h = jnp.where(sub > off + 1, h, 0.0)
                base = jnp.where(sub > off + 1, base, rows[g])
            first[g], second[g] = f, h
            rows[g] = base - f * top - h * low
    full = jnp.concatenate(rows, axis=0)
    i = lax.broadcasted_iota(jnp.int32, (T, T), 0)
    j = lax.broadcasted_iota(jnp.int32, (T, T), 1)
    odd = i % 2 == 1
    pivots = jnp.broadcast_to(jnp.sum(jnp.where(i == j, full, 0.0), axis=1, keepdims=True), (T, T))
    below = jnp.sum(jnp.where(odd & (j == i - 1), full, 0.0), axis=1, keepdims=True)
    unit = jnp.where(j < i - i % 2, full, jnp.where(i == j, 1.0, 0.0))
    ratio = jnp.where(odd, below / pltpu.roll(pivots, 1, axis=0), 0.0)
    return (unit - ratio * pltpu.roll(unit, 1, axis=0)) * lax.rsqrt(pivots - below * ratio)


MESH = pl.DeviceIdType.MESH
SIDE = 4
SLICES = 1
ORDERS = (("x", "y", "z"), ("y", "z", "x"), ("z", "x", "y"))

def place():
    r, d = lax.axis_index("range"), lax.axis_index("doppler")
    return {"z": r // SIDE, "y": r % SIDE, "x": d // 2, "c": d % 2}

def device(at):
    return (at["z"] * SIDE + at["y"], at["x"] * 2 + at["c"])

def moved(at, axis, step):
    return {**at, axis: (at[axis] + step) % SIDE}

def twin(at):
    return {**at, "c": 1 - at["c"]}

def greet(at):
    barrier = pltpu.get_barrier_semaphore()
    friends = [moved(at, a, s) for a in "xyz" for s in range(1, SIDE)] + [twin(at)]
    for friend in friends:
        pl.semaphore_signal(barrier, inc=1, device_id=device(friend), device_id_type=MESH)
    pl.semaphore_wait(barrier, len(friends))

HALF = 64
PACKED = 200
CUT = 104
TOP, LOW, ALL = (0, CUT), (CUT, PACKED - CUT), (0, PACKED)
REDUCE = (("z", "y", "x"), ("x", "z", "y"), ("y", "x", "z"))

def cross(a, b):
    return lax.dot_general(a, b, (((0,), (0,)), ((), ())), preferred_element_type=jnp.float32)

def packed_part(part, snaps):
    first, second, third = snaps[:, :T], snaps[:, T:2 * T], snaps[:, 2 * T:]
    i = lax.broadcasted_iota(jnp.int32, (HALF, T), 0)
    j = lax.broadcasted_iota(jnp.int32, (HALF, T), 1)
    if part == 2:
        both = cross(third, jnp.concatenate([first, third], axis=1))
        tile, square = both[:, :T], both[:, T:]
        turned = pltpu.roll(square[:HALF], HALF, axis=1)
        fold = jnp.where(j - HALF > i, turned, square[HALF:])
        ridge = jnp.where(j - HALF == i, turned, 0.0)
    else:
        lo = part * HALF
        lower = cross(first, first)[lo:lo + HALF]
        if part == 0:
            both = cross(second, snaps[:, :2 * T])
            tile, upper = both[:, :T], both[lo:lo + HALF, T:]
        else:
            both = cross(second, snaps[:, T:])
            tile, upper = both[:, T:], both[lo:lo + HALF, :T]
        fold = jnp.where(j <= i + lo, lower, upper)
        ridge = jnp.where(j == i + lo, upper, 0.0)
    return tile, fold, jnp.broadcast_to(jnp.sum(ridge, axis=0, keepdims=True), (8, T))

def unpack(packed, roll):
    i = lax.broadcasted_iota(jnp.int32, (T, T), 0)
    j = lax.broadcasted_iota(jnp.int32, (T, T), 1)
    fold = jnp.concatenate([packed[0, T:T + HALF], packed[1, T:T + HALF]], axis=0)
    ridge = packed[0, PACKED - 8:PACKED - 7] + packed[1, PACKED - 8:PACKED - 7]
    t00 = jnp.where(j <= i, fold, fold.T)
    t11 = jnp.where(j > i, fold, jnp.where(i == j, ridge, fold.T))
    low = packed[2, T:T + HALF]
    mixed = jnp.concatenate([roll(low, HALF, 1), low], axis=0)
    ridge = roll(packed[2, PACKED - 8:], HALF, 1)[:1]
    keep = ((i < HALF) & (j < HALF) & (j > i)) | ((i >= HALF) & (j <= i))
    t22 = jnp.where((i == j) & (i < HALF), ridge, jnp.where(keep, mixed, mixed.T))
    return t00, packed[0, :T], t11, packed[2, :T], packed[1, :T].T, t22

def reduce_phase(at, count_ref, snap_ref, order_ref, out_ref, go, own, other, marks, grams, far1, down1, up1, far2, down2, up2, far3, down3, up3,
                  own_sem, twin_send, twin_recv, mark_send, mark_recv, send1, recv1, send2, recv2):
    twin_at = twin(at)
    me = ((at["z"] * SIDE + at["y"]) * SIDE + at["x"]) * 2
    far = (far1, far2, far3)
    down_in = (down1, down2, down3)
    up_in = (up1, up2, up3)

    def turn(axis, step):
        return (at[axis] + step) % SIDE

    def own_copy(z):
        return pltpu.make_async_copy(snap_ref.at[z, :, :, at["c"]], own.at[z], own_sem.at[z])
    def twin_copy(z):
        return pltpu.make_async_remote_copy(
            src_ref=snap_ref.at[z, :, :, twin_at["c"]], dst_ref=other.at[z], send_sem=twin_send.at[z], recv_sem=twin_recv.at[z],
            device_id=device(twin_at), device_id_type=MESH)
    order = [turn("z", s) for s in (2, 1, 3, 0)]

    def mark_copy(stage, kind):
        ref = marks.at[(at["z"], at["y"], at["x"])[:SIDE - 1 - stage]]
        target = moved(at, "xyz"[stage], kind + 1)
        return pltpu.make_async_remote_copy(
            src_ref=ref, dst_ref=ref, send_sem=mark_send.at[stage, kind], recv_sem=mark_recv.at[stage, kind],
            device_id=device(target), device_id_type=MESH)
    for z in order:
        twin_copy(z).start()
        own_copy(z).start()
    marks[at["z"], at["y"], at["x"]] = selection(order_ref[...], count_ref[0])
    for stage in range(3):
        for kind in range(3):
            mark_copy(stage, kind).start()
        for kind in range(3):
            mark_copy(stage, kind).wait_recv()
    for stage in range(3):
        for kind in range(3):
            mark_copy(stage, kind).wait_send()

    lane = lax.broadcasted_iota(jnp.int32, (1, T), 1)
    def ready(z):
        own_copy(z).wait()
        twin_copy(z).wait_recv()
        def mask(n, carry):
            y, x = n // SIDE, n % SIDE
            row = marks[z, y, x][:1]
            for ref, block in ((own, me + at["c"]), (other, me + twin_at["c"])):
                keep = jnp.sum(jnp.where(lane == block, row, 0.0), axis=1, keepdims=True)
                keep = jnp.broadcast_to(keep, (1, ref.shape[-1])).astype(jnp.bfloat16)
                ref[z, y, x] = ref[z, y, x] * keep
            return carry
        lax.fori_loop(0, SIDE * SIDE, mask, 0, unroll=4)

    def compute(part, i3, i2):
        names = REDUCE[part]
        def one(i1, carry):
            where = dict(zip(names, (i3, i2, i1)))
            spot = (where["z"], where["y"], where["x"])
            snaps = jnp.concatenate([own[spot], other[spot]], axis=0)
            tile, fold, ridge = packed_part(part, snaps)
            grams[part, i3, i2, i1, 0:T] = tile
            grams[part, i3, i2, i1, T:T + HALF] = fold
            grams[part, i3, i2, i1, T + HALF:PACKED] = ridge
            return carry
        lax.fori_loop(0, SIDE, one, 0, unroll=True)

    KIND = (
        (2, TOP, "far", 1), (2, LOW, "far", SIDE - 1), (1, LOW, "near", 1),
        (SIDE - 1, TOP, "near", SIDE - 1), (1, TOP, "near", 1), (SIDE - 1, LOW, "near", SIDE - 1),
    )
    def hop(part, stage, kind, chunk=None):
        step, (lo, count), slot, way = KIND[kind]
        names = REDUCE[part]
        prefix = tuple(at[a] for a in names[:stage])
        tail = () if chunk is None else (chunk,)
        rows = (slice(None),) * (2 - stage - len(tail)) + (pl.ds(lo, count), slice(None))
        src = grams.at[(part,) + prefix + (turn(names[stage], step),) + tail + rows]
        box = far[stage] if slot == "far" else (down_in[stage] if way == 1 else up_in[stage])
        dst = box.at[(part,) + tail + rows]
        if chunk is None:
            ss, rs = send2.at[part, stage - 1, kind], recv2.at[part, stage - 1, kind]
        else:
            ss, rs = send1.at[part, kind, chunk], recv1.at[part, kind, chunk]
        return pltpu.make_async_remote_copy(
            src_ref=src, dst_ref=dst, send_sem=ss, recv_sem=rs,
            device_id=device(moved(at, names[stage], way)), device_id_type=MESH)

    def add_far(part, stage, kind, chunk=None):
        names = REDUCE[part]
        prefix = tuple(at[a] for a in names[:stage])
        tail = () if chunk is None else (chunk,)
        step, (lo, count) = (1, TOP) if kind == 0 else (SIDE - 1, LOW)
        whole = (slice(None),) * (2 - stage - len(tail)) + (slice(lo, lo + count), slice(None))
        spot = (part,) + prefix + (turn(names[stage], step),) + tail + whole
        grams[spot] = grams[spot] + far[stage][(part,) + tail + whole]

    def add_near(part, stage, chunk=None):
        names = REDUCE[part]
        tail = () if chunk is None else (chunk,)
        spot = (part,) + tuple(at[a] for a in names[:stage + 1]) + tail
        got = (part,) + tail
        grams[spot] = grams[spot] + down_in[stage][got] + up_in[stage][got]

    def second(part, q):
        return (at[REDUCE[part][1]] + 6 - q) % SIDE

    def loop(body):
        def run(q, carry):
            body(q)
            return carry
        lax.fori_loop(0, SIDE, run, 0)

    leads = at["c"] == 0

    def compute_first(part, i3, i2):
        pl.when(leads)(lambda: compute(part, i3, i2))

    def far_out(part):
        def body(q):
            compute_first(part, turn(REDUCE[part][0], 2), second(part, q))
            hop(part, 0, 0, second(part, q)).start()
            hop(part, 0, 1, second(part, q)).start()
        loop(body)

    ready(order[0])
    pl.when(leads)(lambda: far_out(0))
    for z in order[1:]:
        ready(z)

    @pl.when(jnp.logical_not(leads))
    def _():
        for part in range(3):
            def every(n, carry):
                compute(part, n // SIDE, n % SIDE)
                return carry
            lax.fori_loop(0, SIDE * SIDE, every, 0)
        pl.semaphore_wait(go, 1)
        far_out(0)

    far_out(1)
    far_out(2)

    def near_out(q):
        for part in range(3):
            for step, kind in ((1, 2), (SIDE - 1, 3)):
                compute_first(part, turn(REDUCE[part][0], step), second(part, q))
                hop(part, 0, kind, second(part, q)).start()
    loop(near_out)

    def relay(q):
        for part in range(3):
            compute_first(part, at[REDUCE[part][0]], second(part, q))
        for part in range(3):
            chunk = second(part, q)
            for kind in (0, 1):
                hop(part, 0, kind, chunk).wait_recv()
                add_far(part, 0, kind, chunk)
                hop(part, 0, kind + 4, chunk).start()
    loop(relay)

    for q in range(SIDE):
        for part in range(3):
            chunk = second(part, q)
            for kind in (2, 3, 4, 5):
                hop(part, 0, kind, chunk).wait_recv()
            add_near(part, 0, chunk)
            for kind in ((0, 1), (2,), (), (3,))[q]:
                hop(part, 1, kind).start()
    @pl.when(leads)
    def _():
        pl.semaphore_signal(go, inc=1, device_id=device(twin_at), device_id_type=MESH)

    for stage in (1, 2):
        for part in range(3):
            for kind in (0, 1):
                hop(part, stage, kind).wait_recv()
                add_far(part, stage, kind)
                hop(part, stage, kind + 4).start()
        for part in range(3):
            for kind in (2, 3, 4, 5):
                hop(part, stage, kind).wait_recv()
            add_near(part, stage)
            if stage == 1:
                for kind in range(4):
                    hop(part, 2, kind).start()
    for part in range(3):
        out_ref[part] = grams[(part,) + tuple(at[a] for a in REDUCE[part])]

    for z in order:
        twin_copy(z).wait_send()
    def drain(q):
        for part in range(3):
            for kind in range(6):
                hop(part, 0, kind, q).wait_send()
    loop(drain)
    for part in range(3):
        for stage in (1, 2):
            for kind in range(6):
                hop(part, stage, kind).wait_send()


def solve_phase(count_ref, packed, steer_ref, out_ref, diag, cov, rhs, inv):
    n = cov.shape[0] // T
    scale = (BLOCK * count_ref[0]).astype(jnp.float32)
    i = lax.broadcasted_iota(jnp.int32, (T, T), 0)
    j = lax.broadcasted_iota(jnp.int32, (T, T), 1)
    tiles = unpack(packed, pltpu.roll)
    for (r, c), tile in zip(((0, 0), (1, 0), (1, 1), (2, 0), (2, 1), (2, 2)), tiles):
        tile = tile / scale
        if r == c:
            diag[r] = tile + jnp.where(i == j, LOADING, 0.0)
        else:
            cov[r * T:(r + 1) * T, c * T:(c + 1) * T] = tile
    rhs[...] = steer_ref[...].astype(jnp.float32)

    def forward(b, carry):
        inv[b] = factor_inverse(diag[b])
        for which in range(n):
            def update(b=which):
                lo, hi = b * T, (b + 1) * T
                li = inv[b]
                y = mm(li, rhs[lo:hi, :], 1, 0)
                rhs[lo:hi, :] = y
                if b + 1 < n:
                    panel = mm(cov[hi:, lo:hi], li, 1, 1)
                    cov[hi:, lo:hi] = panel
                    diag[b + 1] = diag[b + 1] - mm(panel[:T], panel[:T], 1, 1)
                    rhs[hi:, :] = rhs[hi:, :] - mm(panel, y, 1, 0)
                if b + 2 < n:
                    diag[b + 2] = diag[b + 2] - mm(panel[T:], panel[T:], 1, 1)
                    cov[hi + T:, hi:hi + T] = cov[hi + T:, hi:hi + T] - mm(panel[T:], panel[:T], 1, 1)
            pl.when(b == which)(update)
        return carry
    lax.fori_loop(0, n, forward, 0)
    for b in reversed(range(n)):
        lo, hi = b * T, (b + 1) * T
        y = rhs[lo:hi, :]
        if b + 1 < n:
            y = y - mm(cov[hi:, lo:hi], rhs[hi:, :], 0, 0)
        rhs[lo:hi, :] = mm(inv[b], y, 0, 0)
    solved = rhs[...]
    response = jnp.sum(steer_ref[...].astype(jnp.float32) * solved, axis=0, keepdims=True)
    out_ref[...] = (solved / response).astype(out_ref.dtype)


def gather_phase(at, own_ref, all_ref, local_sem, send_sem, recv_sem, twin_send, twin_recv):
    rows = own_ref.shape[0] // (3 * SLICES)
    half = rows // 2

    def window(part, gathered, where, halves):
        lo, count = (part * rows, rows) if halves is None else (part * rows + halves * half, half)
        pick = tuple(slice(None) if a in gathered else where[a] for a in "zyx")
        return all_ref.at[pick + (where["c"], pl.ds(lo, count), slice(None))]

    def copy(part, stage, kind, gathered, where, halves, target, send, recv, src=None):
        ref = window(part, gathered, where, halves)
        return pltpu.make_async_remote_copy(
            src_ref=ref if src is None else src, dst_ref=ref, send_sem=send.at[part, stage, kind], recv_sem=recv.at[part, stage, kind],
            device_id=device(target), device_id_type=MESH)

    pending, shared = [], []
    def send(part, stage, kind, gathered, where, halves, target):
        src = own_ref.at[pl.ds(part * rows + halves * half, half)] if stage == 0 else None
        one = copy(part, stage, kind, gathered, where, halves, target, send_sem, recv_sem, src)
        one.start()
        pending.append(one)
    def arrive(part, stage, kind, gathered, where, halves):
        copy(part, stage, kind, gathered, where, halves, twin(at), send_sem, recv_sem).wait_recv()
    def share(part, stage, kind, gathered, where, halves):
        one = copy(part, stage, kind, gathered, where, halves, twin(at), twin_send, twin_recv)
        one.start()
        shared.append((one, part, stage, kind, gathered, where, halves))

    def around(part, stage):
        names = ORDERS[part // SLICES]
        axis, gathered = names[stage], names[:stage]
        return gathered, moved(at, axis, 1), moved(at, axis, SIDE - 1), moved(at, axis, 2)
    def begin(part, stage):
        gathered, up, down, far = around(part, stage)
        send(part, stage, 0, gathered, at, 0, up)
        send(part, stage, 1, gathered, at, 1, down)
        send(part, stage, 2, gathered, at, 1, up)
        send(part, stage, 3, gathered, at, 0, down)
        if stage == 0:
            send(part, stage, 4, gathered, at, 0, far)
            send(part, stage, 5, gathered, at, 1, far)
    def relay(part, stage):
        gathered, up, down, _ = around(part, stage)
        arrive(part, stage, 0, gathered, down, 0)
        if stage:
            send(part, stage, 4, gathered, down, 0, up)
        share(part, stage, 0, gathered, down, 0)
        arrive(part, stage, 1, gathered, up, 1)
        if stage:
            send(part, stage, 5, gathered, up, 1, down)
        share(part, stage, 1, gathered, up, 1)
    def finish(part, stage, kinds):
        gathered, up, down, far = around(part, stage)
        for kind in kinds:
            where, halves = ((down, 1), (up, 0), (far, 0), (far, 1))[kind - 2]
            arrive(part, stage, kind, gathered, where, halves)
            share(part, stage, kind, gathered, where, halves)

    parts = [[axis * SLICES + piece for axis in range(3)] for piece in range(SLICES)]
    local = pltpu.make_async_copy(own_ref, all_ref.at[at["z"], at["y"], at["x"], at["c"]], local_sem)
    local.start()
    for group in parts:
        for part in group:
            begin(part, 0)
    local.wait()
    for part in range(3 * SLICES):
        share(part, 3, 0, (), at, None)
    for stage in range(3):
        for group in parts:
            for part in group:
                relay(part, stage)
            for part in group:
                finish(part, stage, (2, 3))
            for part in group:
                finish(part, stage, (4, 5))
                if stage < 2:
                    begin(part, stage + 1)
    for one in pending:
        one.wait_send()
    for one, part, stage, kind, gathered, where, halves in shared:
        one.wait_send()
        copy(part, stage, kind, gathered, twin(where), halves, twin(at), twin_send, twin_recv).wait_recv()


def adapt_kernel(count_ref, snap_ref, order_ref, steer_ref, all_ref, packed, weights, diag, cov, rhs, inv, go, *scratch):
    at = place()
    greet(at)
    reduce_phase(at, count_ref, snap_ref, order_ref, packed, go, *scratch[:-5])
    solve_phase(count_ref, packed, steer_ref, weights, diag, cov, rhs, inv)
    gather_phase(at, weights, all_ref, *scratch[-5:])


def adapt(snapshots, train_list, train_count, steering):
    bins, gates, channels = snapshots.shape
    looks = steering.shape[1]
    split = snapshots.reshape(SIDE, SIDE, SIDE, 2, gates, channels)
    f32, bf16, sem = jnp.float32, jnp.bfloat16, pltpu.SemaphoreType.DMA
    boxes = [pltpu.VMEM((3,) + (SIDE,) * n + (PACKED, T), f32) for n in (2, 2, 2, 1, 1, 1, 0, 0, 0)]
    vmem = pl.BlockSpec(memory_space=pltpu.VMEM)
    whole = pl.pallas_call(
        adapt_kernel,
        out_shape=jax.ShapeDtypeStruct((SIDE, SIDE, SIDE, 2, channels, looks), bf16),
        in_specs=[pl.BlockSpec(memory_space=pltpu.SMEM), pl.BlockSpec(memory_space=pl.ANY), vmem, vmem],
        out_specs=pl.BlockSpec(memory_space=pl.ANY),
        scratch_shapes=[
            pltpu.VMEM((3, PACKED, T), f32), pltpu.VMEM((channels, looks), bf16), pltpu.VMEM((channels // T, T, T), f32),
            pltpu.VMEM((channels, channels), f32), pltpu.VMEM((channels, looks), f32), pltpu.VMEM((channels // T, T, T), f32),
            pltpu.SemaphoreType.REGULAR,
            pltpu.VMEM((SIDE, SIDE, SIDE, gates, channels), bf16), pltpu.VMEM((SIDE, SIDE, SIDE, gates, channels), bf16),
            pltpu.VMEM((SIDE, SIDE, SIDE, 8, T), f32), pltpu.VMEM((3, SIDE, SIDE, SIDE, PACKED, T), f32), *boxes,
            sem((SIDE,)), sem((SIDE,)), sem((SIDE,)), sem((3, 3)), sem((3, 3)),
            sem((3, 6, SIDE)), sem((3, 6, SIDE)), sem((3, 2, 6)), sem((3, 2, 6)),
            sem, *[sem((3 * SLICES, n, 6)) for n in (3, 3, 4, 4)],
        ],
        compiler_params=pltpu.CompilerParams(collective_id=1, has_side_effects=True, vmem_limit_bytes=67000000),
        name="adapt",
    )(train_count, split, train_list, steering)
    return whole.reshape(bins, channels, looks)


def apply_kernel(snap_hbm, weight_hbm, out_hbm, snaps, weights, outs, snap_sem, weight_sem, out_sem):
    chunks = snap_sem.shape[0]
    step = snaps.shape[0] // chunks

    def part(n):
        return pl.ds(pl.multiple_of(n * step, step), step)
    def snap_copy(n):
        return pltpu.make_async_copy(snap_hbm.at[part(n)], snaps.at[part(n)], snap_sem.at[n])
    def weight_copy(n):
        return pltpu.make_async_copy(weight_hbm.at[part(n)], weights.at[part(n)], weight_sem.at[n])
    def out_copy(n):
        return pltpu.make_async_copy(outs.at[part(n)], out_hbm.at[part(n)], out_sem.at[n])

    def fetch(n, carry):
        snap_copy(n).start()
        weight_copy(n).start()
        return carry
    lax.fori_loop(0, chunks, fetch, 0)
    def multiply(n, carry):
        snap_copy(n).wait()
        weight_copy(n).wait()
        for b in range(step):
            at = n * step + b
            outs[at] = jnp.dot(snaps[at], weights[at], preferred_element_type=jnp.float32).astype(outs.dtype)
        out_copy(n).start()
        return carry
    lax.fori_loop(0, chunks, multiply, 0)
    def drain(n, carry):
        out_copy(n).wait()
        return carry
    lax.fori_loop(0, chunks, drain, 0)


def beams(snapshots, weights, chunks=16):
    bins, gates, channels = snapshots.shape
    looks = weights.shape[2]
    bf16, sem, whole = jnp.bfloat16, pltpu.SemaphoreType.DMA, pl.BlockSpec(memory_space=pl.ANY)
    return pl.pallas_call(
        apply_kernel,
        out_shape=jax.ShapeDtypeStruct((bins, gates, looks), bf16),
        in_specs=[whole, whole],
        out_specs=whole,
        scratch_shapes=[
            pltpu.VMEM((bins, gates, channels), bf16), pltpu.VMEM((bins, channels, looks), bf16), pltpu.VMEM((bins, gates, looks), bf16),
            sem((chunks,)), sem((chunks,)), sem((chunks,)),
        ],
        compiler_params=pltpu.CompilerParams(vmem_limit_bytes=60 * 1024 * 1024),
        name="beams",
    )(snapshots, weights)


def body(snapshots, steering, train_list, train_count):
    weights = adapt(snapshots, train_list, train_count, steering[0])
    return beams(snapshots, weights)


def solution(mesh):
    placed = (
        P(None, ("range", "doppler"), None),
        P(("range", "doppler"), None, None),
        P(("range", "doppler"), None),
        P(("range", "doppler")),
    )
    return jax.shard_map(
        body,
        mesh=mesh,
        in_specs=placed,
        out_specs=P(None, ("range", "doppler"), None),
        check_vma=False,
    )
```
